128 devices in a mesh: dp: 16 (over x, y), space: 8 (over z, core).
Axes of the slice: x: 4, y: 4, z: 4, core: 2. Of those that a mesh axis runs over, the one named last changes fastest.
Arguments:
- features: bfloat16 [16, 24576, 128], P('dp', 'space'), may hold values from -6 to 6
- neighbours: int32 [16, 27, 24576], P('dp', None, 'space'), may hold values from -1 to 24575, as said below
- weight: bfloat16 [27, 128, 128], replicated, may hold values from -0.109375 to 0.109375
- grad_out: bfloat16 [16, 24576, 128], P('dp', 'space'), may hold values from -6 to 6
Outputs:
- conv_out: bfloat16 [16, 24576, 128], P('dp', 'space')
- grad_in: bfloat16 [16, 24576, 128], P('dp', 'space')
- grad_w: float32 [27, 128, 128], replicated
The draws below stay inside these ranges and needn't reach their ends.
Inputs may be any that keep to these rules, and one draw needn't show every extreme that they name: Voxels of a scene are ordered by layer, 1024 per layer and layer z holding indices z * 1024 to (z + 1) * 1024 - 1; within a layer they are ordered by cell y * 64 + x, and every grid row y of every layer holds exactly 16 active voxels, so row y of layer z holds indices z * 1024 + y * 16 onward. An entry for offset (dz, dy, dx) of a voxel in layer z, row y points into layer z + dz, row y + dy. The map is symmetric: neighbours[26 - k, neighbours[k, i]] = i wherever neighbours[k, i] >= 0, and neighbours[13, i] = i.
All inputs are finite; a program needn't handle non-finite values.
Results may differ from the reference program's by a relative error of at most 0.0055.
Values may be sent and summed in bfloat16 or wider, within the bound.
A program may use at most 64 MiB of HBM per device.

```python
import math
import jax
import jax.numpy as jnp
from jax import lax

C = 128
KVOL = 27
PSIDE = 64
NZ = 24
VOX_S = 24576
SCENES = 16
N_DP = 16


def draw_neighbours(key, part):
    plane = PSIDE * PSIDE
    per_row = PSIDE // 4
    layer_size = plane // 4

    def one_scene(scene_key):
        layer_keys = jax.random.split(scene_key, NZ)

        def pick_cells(layer_key):
            row_keys = jax.random.split(layer_key, PSIDE)

            def pick_row(row_key):
                shuffled = jax.random.permutation(row_key, PSIDE)
                return jnp.sort(shuffled[:per_row]).astype(jnp.int32)
            columns = jax.vmap(pick_row)(row_keys)
            row_base = (jnp.arange(PSIDE, dtype=jnp.int32) * PSIDE)[:, None]
            return (columns + row_base).reshape(-1).astype(jnp.int32)
        cells = jax.vmap(pick_cells)(layer_keys)
        layer_ids = jnp.arange(NZ, dtype=jnp.int32)[:, None]
        ranks = jnp.full((NZ, plane), -1, jnp.int32)
        ranks = ranks.at[jnp.broadcast_to(layer_ids, (NZ, layer_size)), cells].set(jnp.broadcast_to(jnp.arange(layer_size, dtype=jnp.int32)[None, :], (NZ, layer_size)))
        pos_z = jnp.broadcast_to(layer_ids, (NZ, layer_size))
        pos_y = cells // PSIDE
        pos_x = cells % PSIDE
        kernel_maps = []
        for step_z in (-1, 0, 1):
            for step_y in (-1, 0, 1):
                for step_x in (-1, 0, 1):
                    near_z = pos_z + step_z
                    near_y = pos_y + step_y
                    near_x = pos_x + step_x
                    inside = (near_z >= 0) & (near_z < NZ) & (near_y >= 0) & (near_y < PSIDE) & (near_x >= 0) & (near_x < PSIDE)
                    clip_z = jnp.clip(near_z, 0, NZ - 1)
                    clip_y = jnp.clip(near_y, 0, PSIDE - 1)
                    clip_x = jnp.clip(near_x, 0, PSIDE - 1)
                    found = ranks[clip_z, clip_y * PSIDE + clip_x]
                    target = jnp.where(inside & (found >= 0), clip_z * layer_size + found, -1)
                    kernel_maps.append(target.reshape(-1))
        return jnp.stack(kernel_maps).astype(jnp.int32)
    scene_keys = jax.random.split(key, SCENES)
    return jax.vmap(one_scene)(scene_keys)


def levels(stream_key, dims, shards, least, high):
    factor_of, own = 1.0, jax.random.fold_in(stream_key, 6)
    for position, parts in shards:
        steps = jnp.exp(jax.random.uniform(jax.random.fold_in(own, position), (parts,), jnp.float32, least / len(shards), high / len(shards)))
        factor_of = factor_of * jnp.repeat(steps, dims[position] // parts).reshape([-1 if axis == position else 1 for axis in range(len(dims))])
    return factor_of


def gaussian(rng, extent, spread, bound, pieces=(), kind=jnp.bfloat16):
    entries = jax.random.normal(rng, extent, jnp.float32) * spread
    if len(pieces) > 0:
        entries = levels(rng, extent, pieces, -0.22, 0.18) * entries
    return jnp.clip(entries, min=-bound, max=bound).astype(kind)


def setup_inputs(seed: int = 0) -> dict:
    seeds = jax.random.split(jax.random.key(seed), 5)
    return {
        "features": gaussian(seeds[0], (SCENES, VOX_S, C), 1.0, 6.0, ((0, 16), (1, 8))),
        "neighbours": draw_neighbours(jax.random.fold_in(seeds[4], 71), 0),
        "weight": gaussian(seeds[2], (KVOL, C, C), (KVOL * C) ** -0.5, 0.109375),
        "grad_out": gaussian(seeds[3], (SCENES, VOX_S, C), 1.0, 6.0, ((0, 16), (1, 8))),
    }


def conv_scene(feats, neigh_map, weight, grads):
    voxels = feats.shape[0]
    channels = feats.shape[1]
    zero_row = jnp.zeros((1, channels), feats.dtype)
    extended = jnp.concatenate([feats, zero_row], 0)
    grad_ext = jnp.concatenate([grads, zero_row], 0)
    row_index = jnp.where(neigh_map >= 0, neigh_map, voxels).astype(jnp.int32)
    zero_acc = jnp.zeros((voxels, channels), jnp.float32)

    def forward_step(total, pair_item):
        index_row, kernel = pair_item
        picked = jnp.take(extended, index_row, axis=0)
        return (total + jnp.dot(picked, kernel, preferred_element_type=jnp.float32), None)
    result, _ = lax.scan(forward_step, zero_acc, (row_index, weight))

    def backward_step(total, pair_item):
        index_row, kernel = pair_item
        picked = jnp.take(grad_ext, index_row, axis=0)
        return (total + lax.dot_general(picked, kernel, (((1,), (1,)), ((), ())), preferred_element_type=jnp.float32), None)
    grad_x, _ = lax.scan(backward_step, zero_acc, (row_index[::-1], weight))

    def weight_term(index_row):
        picked = jnp.take(extended, index_row, axis=0)
        return lax.dot_general(picked, grads, (((0,), (0,)), ((), ())), preferred_element_type=jnp.float32)
    weight_terms = lax.map(weight_term, row_index)
    return (result.astype(jnp.bfloat16), grad_x.astype(jnp.bfloat16), weight_terms)

def reference(features, neighbours, weight, grad_out):

    def per_scene(scene_item):
        return conv_scene(scene_item[0], scene_item[1], weight, scene_item[2])
    conv_out, grad_in, weight_terms = lax.map(per_scene, (features, neighbours, grad_out))
    norm_factor = 1.0 / math.sqrt(N_DP * VOX_S)
    grad_w = lax.optimization_barrier(jnp.sum(weight_terms, axis=0)) * norm_factor
    return (conv_out, grad_in, grad_w)
```

```python
import functools
import math

import jax
import jax.numpy as jnp
from jax import lax
from jax.experimental import pallas as pl
from jax.experimental.pallas import tpu as pltpu
from jax.sharding import PartitionSpec as P

LAYER, ROW, TAPS, C, TILE = 1024, 16, 27, 128, 128
PAD = ROW
bf16 = jnp.bfloat16


def one_hot(targets, first):
    local = jnp.where(targets >= 0, targets - first, -1)
    local = jnp.where((local >= 0) & (local < TILE), local, -1)
    local = local.astype(jnp.float32).astype(bf16)
    rows = lax.broadcasted_iota(jnp.int32, (TILE, TILE), 0).astype(jnp.float32).astype(bf16)
    return jnp.where(
        jnp.broadcast_to(local, (TILE, TILE)) == rows, jnp.ones((), bf16), jnp.zeros((), bf16)
    )


def scatter_tile(feats, grads, targets, first_target, row, tap0, picked_f, picked_g):
    hot = [
        one_hot(targets[t : t + 1], first_target + (t // 3 - 1) * ROW) for t in range(9)
    ]
    out = jnp.dot(
        jnp.concatenate(hot, 0),
        jnp.concatenate([feats, grads], 1),
        preferred_element_type=jnp.float32,
    ).astype(bf16)
    for t in range(9):
        k = tap0 + t
        at = pl.ds(pl.multiple_of(row + (t // 3 - 1) * ROW, ROW), TILE)
        picked_f[at, k * C : (k + 1) * C] = out[t * TILE : (t + 1) * TILE, :C]
        picked_g[at, k * C : (k + 1) * C] = out[t * TILE : (t + 1) * TILE, C:]


def conv_kernel(
    base_ref, f_ref, g_ref, n_ref, flo, fhi, glo, ghi, nlo, nhi, w_ref,
    conv_ref, gin_ref, gw_ref, picked_f, picked_g, f_t,
    *, voxels, unroll, rows,
):
    base = base_ref[0]
    tiles, layer_tiles = voxels // TILE, LAYER // TILE
    for row in (0, ROW, voxels + PAD - ROW, voxels + PAD):
        picked_f[row : row + ROW, :] = jnp.zeros((ROW, TAPS * C), bf16)
        picked_g[row : row + ROW, :] = jnp.zeros((ROW, TAPS * C), bf16)

    @pl.loop(0, tiles)
    def _(i):
        at = pl.ds(pl.multiple_of(i * TILE, TILE), TILE)
        f_t[:, at] = f_ref[at, :].T

    def each(count, body):
        @pl.loop(0, count // unroll)
        def _(i):
            for u in range(unroll):
                body(i * unroll + u)

    def own(t, dz):
        start = pl.multiple_of(t * TILE, TILE)
        at = pl.ds(start, TILE)
        tap0 = 9 * (dz + 1)
        scatter_tile(
            f_ref[at, :], g_ref[at, :], n_ref[tap0 : tap0 + 9, at],
            base + start + dz * LAYER, start + PAD + dz * LAYER, tap0, picked_f, picked_g,
        )

    def halo(t, f, g, n, dz, layer):
        start = pl.multiple_of(t * TILE, TILE)
        at = pl.ds(start, TILE)
        scatter_tile(
            f[at, :], g[at, :], n[:, at],
            base + layer * LAYER + start, start + PAD + layer * LAYER, 9 * (dz + 1),
            picked_f, picked_g,
        )

    each(tiles, lambda t: own(t, 0))
    each(tiles - layer_tiles, lambda t: own(t, 1))
    each(tiles - layer_tiles, lambda t: own(t + layer_tiles, -1))
    each(layer_tiles, lambda t: halo(t, flo, glo, nlo, 1, 0))
    each(layer_tiles, lambda t: halo(t, fhi, ghi, nhi, -1, voxels // LAYER - 1))

    def weight_grad(k, count):
        at = pl.ds(pl.multiple_of(k * C, C), count * C)
        term = jnp.dot(
            f_t[...], picked_g[PAD : PAD + voxels, at], preferred_element_type=jnp.float32
        )
        for c in range(count):
            gw_ref[k + c] = term[:, c * C : (c + 1) * C]

    @pl.loop(0, TAPS // 2)
    def _(i):
        weight_grad(2 * i, 2)

    weight_grad(TAPS - 1, 1)

    @pl.loop(0, voxels // rows)
    def _(i):
        start = pl.multiple_of(i * rows, rows)
        kernel = jnp.concatenate([w_ref[TAPS - 1 - k] for k in range(TAPS)], 0)
        conv_ref[pl.ds(start, rows), :] = jnp.dot(
            picked_f[pl.ds(start + PAD, rows), :], kernel, preferred_element_type=jnp.float32
        ).astype(bf16)

    @pl.loop(0, voxels // rows)
    def _(i):
        start = pl.multiple_of(i * rows, rows)
        kernel = jnp.concatenate([w_ref[k] for k in range(TAPS)], 1)
        gin_ref[pl.ds(start, rows), :] = lax.dot_general(
            picked_g[pl.ds(start + PAD, rows), :], kernel, (((1,), (1,)), ((), ())),
            preferred_element_type=jnp.float32,
        ).astype(bf16)


def local(features, neighbours, weight, grad_out):
    feats, grads, neigh = features[0], grad_out[0], neighbours[0]
    voxels = feats.shape[0]
    count = lax.axis_size("space")
    up = [(i, i + 1) for i in range(count - 1)]
    down = [(i + 1, i) for i in range(count - 1)]
    flo = lax.ppermute(feats[-LAYER:], "space", up)
    glo = lax.ppermute(grads[-LAYER:], "space", up)
    nlo = lax.ppermute(neigh[18:, -LAYER:], "space", up)
    fhi = lax.ppermute(feats[:LAYER], "space", down)
    ghi = lax.ppermute(grads[:LAYER], "space", down)
    nhi = lax.ppermute(neigh[:9, :LAYER], "space", down)
    base = (lax.axis_index("space") * voxels).astype(jnp.int32).reshape(1)
    vmem = pl.BlockSpec(memory_space=pltpu.VMEM)
    conv, gin, gw = pl.pallas_call(
        functools.partial(conv_kernel, voxels=voxels, unroll=4, rows=1024),
        out_shape=(
            jax.ShapeDtypeStruct((voxels, C), bf16),
            jax.ShapeDtypeStruct((voxels, C), bf16),
            jax.ShapeDtypeStruct((TAPS, C, C), jnp.float32),
        ),
        in_specs=[pl.BlockSpec(memory_space=pltpu.SMEM)] + [vmem] * 10,
        out_specs=(vmem, vmem, vmem),
        scratch_shapes=[
            pltpu.VMEM((voxels + 2 * PAD, TAPS * C), bf16),
            pltpu.VMEM((voxels + 2 * PAD, TAPS * C), bf16),
            pltpu.VMEM((C, voxels), bf16),
        ],
        compiler_params=pltpu.CompilerParams(vmem_limit_bytes=60 * 2**20),
        name="sparse_conv",
    )(base, feats, grads, neigh, flo, fhi, glo, ghi, nlo, nhi, weight)
    norm = 1.0 / math.sqrt(lax.axis_size("dp") * lax.axis_size("space") * voxels)
    grad_w = lax.psum(gw, ("dp", "space")) * norm
    return conv[None], gin[None], grad_w


def solution(mesh):
    in_specs = (P("dp", "space", None), P("dp", None, "space"), P(), P("dp", "space", None))
    out_specs = (P("dp", "space", None), P("dp", "space", None), P())
    return jax.shard_map(local, mesh=mesh, in_specs=in_specs, out_specs=out_specs, check_vma=False)
```

```python
import functools
import math

import jax
import jax.numpy as jnp
from jax import lax
from jax.experimental import pallas as pl
from jax.experimental.pallas import tpu as pltpu
from jax.sharding import PartitionSpec as P

LAYER, ROW, TAPS, C, TILE = 1024, 16, 27, 128, 128
PAD = ROW
GROUPS = 3
GT = TAPS // GROUPS
bf16, f32 = jnp.bfloat16, jnp.float32
MESH = pl.DeviceIdType.MESH


def one_hot(targets, first):
    local = jnp.where(targets >= 0, targets - first, -1)
    local = jnp.where((local >= 0) & (local < TILE), local, -1)
    local = local.astype(f32).astype(bf16)
    rows = lax.broadcasted_iota(jnp.int32, (TILE, TILE), 0).astype(f32).astype(bf16)
    return jnp.where(
        jnp.broadcast_to(local, (TILE, TILE)) == rows, jnp.ones((), bf16), jnp.zeros((), bf16)
    )


def scatter_tile(feats, grads, targets, first_target, row, tap0, picked_f, picked_g):
    hot = [
        one_hot(targets[t], first_target + (t // 3 - 1) * ROW) for t in range(GT)
    ]
    out = jnp.dot(
        jnp.concatenate(hot, 0),
        jnp.concatenate([feats, grads], 1),
        preferred_element_type=f32,
    ).astype(bf16)
    for t in range(GT):
        k = tap0 + t
        at = pl.ds(pl.multiple_of(row + (t // 3 - 1) * ROW, ROW), TILE)
        picked_f[at, k * C : (k + 1) * C] = out[t * TILE : (t + 1) * TILE, :C]
        picked_g[at, k * C : (k + 1) * C] = out[t * TILE : (t + 1) * TILE, C:]


def kernel(
    f_hbm, n_hbm, w_hbm, g_hbm,
    conv_hbm, gin_hbm, gw_hbm,
    f_ref, g_ref, n_ref, w_ref, conv_ref, gin_ref, picked_f, picked_g, f_t,
    n_halo, f_halo, g_halo, part, part_in, summed, summed_in, result,
    load_sem, halo_send, halo_recv, a_send, a_recv, b_send, b_recv, c_send, c_recv, d_send, d_recv,
    out_sem, own_sem,
    *, voxels, n_dp, n_space, unroll, rows,
):
    layers = voxels // LAYER
    tiles, layer_tiles = voxels // TILE, LAYER // TILE
    chunk = C // n_space
    s = lax.axis_index("space")
    q = lax.axis_index("dp")
    base = s * voxels

    loads = [
        pltpu.make_async_copy(src, dst, load_sem.at[i])
        for i, (src, dst) in enumerate(
            [(n_hbm, n_ref), (f_hbm, f_ref), (g_hbm, g_ref), (w_hbm, w_ref)]
        )
    ]
    for load in loads:
        load.start()

    barrier = pltpu.get_barrier_semaphore()
    for d in range(1, n_space):
        pl.semaphore_signal(
            barrier, inc=1, device_id={"space": lax.rem(s + d, n_space)}, device_id_type=MESH
        )
    for d in range(1, n_dp):
        pl.semaphore_signal(
            barrier, inc=1, device_id={"dp": lax.rem(q + d, n_dp)}, device_id_type=MESH
        )

    for row in (0, ROW, voxels + PAD - ROW, voxels + PAD):
        picked_f[row : row + ROW, :] = jnp.zeros((ROW, TAPS * C), bf16)
        picked_g[row : row + ROW, :] = jnp.zeros((ROW, TAPS * C), bf16)
    pl.semaphore_wait(barrier, n_space - 1 + n_dp - 1)

    def halo_copies(side):
        peer = s + 1 if side == 0 else s - 1
        at = pl.ds(voxels - LAYER if side == 0 else 0, LAYER)
        return [
            pltpu.make_async_remote_copy(
                src_ref=src, dst_ref=dst, send_sem=halo_send.at[side, i],
                recv_sem=halo_recv.at[side, i], device_id={"space": peer}, device_id_type=MESH,
            )
            for i, (src, dst) in enumerate(
                [
                    (n_hbm.at[pl.ds(2 * GT if side == 0 else 0, GT), :, at], n_halo.at[side]),
                    (f_hbm.at[at], f_halo.at[side]),
                    (g_hbm.at[at], g_halo.at[side]),
                ]
            )
        ]

    halos = [halo_copies(0), halo_copies(1)]
    has = [s < n_space - 1, s > 0]

    for side in (0, 1):

        @pl.when(has[side])
        def _():
            for copy in halos[side]:
                copy.start()

    for side in (0, 1):

        @pl.when(jnp.logical_not(has[1 - side]))
        def _():
            n_halo[side] = jnp.full(n_halo.shape[1:], -1, jnp.int32)
            f_halo[side] = jnp.zeros(f_halo.shape[1:], bf16)
            g_halo[side] = jnp.zeros(g_halo.shape[1:], bf16)

    for load in loads[:3]:
        load.wait()

    @pl.loop(0, tiles)
    def _(i):
        at = pl.ds(pl.multiple_of(i * TILE, TILE), TILE)
        f_t[:, at] = f_ref[at, :].T

    def each(count, body):
        @pl.loop(0, count // unroll)
        def _(i):
            for u in range(unroll):
                body(i * unroll + u)

    def own(t, dz):
        start = pl.multiple_of(t * TILE, TILE)
        at = pl.ds(start, TILE)
        tap0 = GT * (dz + 1)
        scatter_tile(
            f_ref[at, :], g_ref[at, :], n_ref[tap0 : tap0 + GT, :, at],
            base + start + dz * LAYER, start + PAD + dz * LAYER, tap0, picked_f, picked_g,
        )

    def from_halo(side):
        dz, layer = (1, 0) if side == 0 else (-1, layers - 1)

        @pl.when(has[1 - side])
        def _():
            for copy in halos[side]:
                copy.wait_recv()

        def body(t):
            start = pl.multiple_of(t * TILE, TILE)
            at = pl.ds(start, TILE)
            scatter_tile(
                f_halo[side, at, :], g_halo[side, at, :], n_halo[side, :, :, at],
                base + layer * LAYER + start, start + PAD + layer * LAYER, GT * (dz + 1),
                picked_f, picked_g,
            )

        each(layer_tiles, body)

    def weight_grad(g):
        def term(k, count):
            at = pl.ds(pl.multiple_of(k * C, C), count * C)
            out = jnp.dot(
                f_t[...], picked_g[PAD : PAD + voxels, at], preferred_element_type=f32
            ).astype(bf16)
            for c in range(count):
                part[k + c] = out[:, c * C : (c + 1) * C]

        @pl.loop(0, GT // 2)
        def _(i):
            term(GT * g + 2 * i, 2)

        term(GT * g + GT - 1, 1)

    def owner(g, t):
        return (GT * g + t) % n_dp

    def taps(g):
        return pl.ds(GT * g, GT)

    def a_copy(g, d):
        to = lax.rem(s + d, n_space)
        return pltpu.make_async_remote_copy(
            src_ref=part.at[taps(g), pl.ds(pl.multiple_of(to * chunk, chunk), chunk)],
            dst_ref=part_in.at[d, taps(g)],
            send_sem=a_send.at[g, d], recv_sem=a_recv.at[g, d],
            device_id={"space": to}, device_id_type=MESH,
        )

    def b_copy(g, t):
        o = owner(g, t)
        d = lax.rem(o - q + n_dp, n_dp)
        return pltpu.make_async_remote_copy(
            src_ref=summed.at[GT * g + t], dst_ref=summed_in.at[g, d],
            send_sem=b_send.at[g, t], recv_sem=b_recv.at[g, d],
            device_id={"dp": o}, device_id_type=MESH,
        )

    def mine(g):
        t = lax.rem(q - (GT * g) % n_dp + n_dp, n_dp)
        return t, t < GT

    def b_arrival(g, d):
        return pltpu.make_async_remote_copy(
            src_ref=summed.at[GT * g], dst_ref=summed_in.at[g, d],
            send_sem=b_send.at[g, 0], recv_sem=b_recv.at[g, d],
            device_id={"dp": lax.rem(q + d, n_dp)}, device_id_type=MESH,
        )

    def c_copy(g, t, d):
        return pltpu.make_async_remote_copy(
            src_ref=result.at[GT * g + t], dst_ref=result.at[GT * g + t],
            send_sem=c_send.at[g, d], recv_sem=c_recv.at[GT * g + t],
            device_id={"dp": lax.rem(q + d, n_dp)}, device_id_type=MESH,
        )

    def d_copy(g, d):
        return pltpu.make_async_remote_copy(
            src_ref=result.at[taps(g)],
            dst_ref=gw_hbm.at[taps(g), pl.ds(pl.multiple_of(s * chunk, chunk), chunk)],
            send_sem=d_send.at[g, d], recv_sem=d_recv.at[g, d],
            device_id={"space": lax.rem(s + d, n_space)}, device_id_type=MESH,
        )

    def own_rows(g):
        return pltpu.make_async_copy(
            result.at[taps(g)],
            gw_hbm.at[taps(g), pl.ds(pl.multiple_of(s * chunk, chunk), chunk)],
            own_sem.at[g],
        )

    def stage_a(g):
        for d in range(1, n_space):
            a_copy(g, d).start()

    def stage_b(g):
        for d in range(1, n_space):
            a_copy(g, d).wait_recv()
        here = pl.ds(pl.multiple_of(s * chunk, chunk), chunk)
        for t in range(GT):
            k = GT * g + t
            total = part[k, here, :].astype(f32)
            for d in range(1, n_space):
                total = total + part_in[d, k].astype(f32)
            summed[k] = total
        for t in range(GT):

            @pl.when(q != owner(g, t))
            def _():
                b_copy(g, t).start()

    def stage_c(g):
        t, owns = mine(g)

        @pl.when(owns)
        def _():
            for d in range(1, n_dp):
                b_arrival(g, d).wait_recv()
            total = summed[GT * g + t]
            for d in range(1, n_dp):
                total = total + summed_in[g, d]
            result[GT * g + t] = total.astype(bf16)
            for d in range(1, n_dp):
                c_copy(g, t, d).start()

    def stage_d(g):
        for t in range(GT):

            @pl.when(q != owner(g, t))
            def _():
                c_copy(g, t, 1).wait_recv()

        for d in range(1, n_space):
            d_copy(g, d).start()
        own_rows(g).start()

    def finish(g):
        t, owns = mine(g)
        for d in range(1, n_space):
            d_copy(g, d).wait_recv()
        own_rows(g).wait()
        for d in range(1, n_space):
            a_copy(g, d).wait_send()
            d_copy(g, d).wait_send()
        for tap in range(GT):

            @pl.when(q != owner(g, tap))
            def _():
                b_copy(g, tap).wait_send()

        @pl.when(owns)
        def _():
            for d in range(1, n_dp):
                c_copy(g, t, d).wait_send()

    each(tiles, lambda t: own(t, 0))
    weight_grad(1)
    stage_a(1)
    each(tiles - layer_tiles, lambda t: own(t, 1))
    stage_b(1)
    each(tiles - layer_tiles, lambda t: own(t + layer_tiles, -1))
    stage_c(1)
    from_halo(0)
    weight_grad(2)
    stage_a(2)
    stage_d(1)
    from_halo(1)
    weight_grad(0)
    stage_a(0)
    loads[3].wait()

    def conv(i):
        start = pl.multiple_of(i * rows, rows)
        taps_in = jnp.concatenate([w_ref[TAPS - 1 - k] for k in range(TAPS)], 0)
        conv_ref[pl.ds(start, rows), :] = jnp.dot(
            picked_f[pl.ds(start + PAD, rows), :], taps_in, preferred_element_type=f32
        ).astype(bf16)

    def gin(i):
        start = pl.multiple_of(i * rows, rows)
        taps_out = jnp.concatenate([w_ref[k] for k in range(TAPS)], 1)
        gin_ref[pl.ds(start, rows), :] = lax.dot_general(
            picked_g[pl.ds(start + PAD, rows), :], taps_out, (((1,), (1,)), ((), ())),
            preferred_element_type=f32,
        ).astype(bf16)

    outs = [
        pltpu.make_async_copy(conv_ref, conv_hbm, out_sem.at[0]),
        pltpu.make_async_copy(gin_ref, gin_hbm, out_sem.at[1]),
    ]
    blocks = voxels // rows

    @pl.loop(0, blocks)
    def _(i):
        conv(i)

        @pl.when(i == 0)
        def _():
            stage_b(2)

        @pl.when(i == 1)
        def _():
            stage_c(2)
            stage_b(0)

        @pl.when(i == 2)
        def _():
            stage_d(2)
            stage_c(0)

    outs[0].start()

    @pl.loop(0, blocks)
    def _(i):
        gin(i)

        @pl.when(i == 0)
        def _():
            stage_d(0)

    outs[1].start()
    for side in (0, 1):

        @pl.when(has[side])
        def _():
            for copy in halos[side]:
                copy.wait_send()

    for g in (1, 2, 0):
        finish(g)
    outs[0].wait()
    outs[1].wait()


def local(features, neighbours, weight, grad_out):
    voxels = features.shape[1]
    n_dp, n_space = lax.axis_size("dp"), lax.axis_size("space")
    chunk = C // n_space
    dma = pltpu.SemaphoreType.DMA
    anywhere = pl.BlockSpec(memory_space=pl.ANY)
    conv, gin, gw = pl.pallas_call(
        functools.partial(
            kernel, voxels=voxels, n_dp=n_dp, n_space=n_space, unroll=4, rows=1024
        ),
        out_shape=(
            jax.ShapeDtypeStruct((voxels, C), bf16),
            jax.ShapeDtypeStruct((voxels, C), bf16),
            jax.ShapeDtypeStruct((TAPS, C, C), bf16),
        ),
        in_specs=[anywhere] * 4,
        out_specs=(anywhere,) * 3,
        scratch_shapes=[
            pltpu.VMEM((voxels, C), bf16),
            pltpu.VMEM((voxels, C), bf16),
            pltpu.VMEM((TAPS, 1, voxels), jnp.int32),
            pltpu.VMEM((TAPS, C, C), bf16),
            pltpu.VMEM((voxels, C), bf16),
            pltpu.VMEM((voxels, C), bf16),
            pltpu.VMEM((voxels + 2 * PAD, TAPS * C), bf16),
            pltpu.VMEM((voxels + 2 * PAD, TAPS * C), bf16),
            pltpu.VMEM((C, voxels), bf16),
            pltpu.VMEM((2, GT, 1, LAYER), jnp.int32),
            pltpu.VMEM((2, LAYER, C), bf16),
            pltpu.VMEM((2, LAYER, C), bf16),
            pltpu.VMEM((TAPS, C, C), bf16),
            pltpu.VMEM((n_space, TAPS, chunk, C), bf16),
            pltpu.VMEM((TAPS, chunk, C), f32),
            pltpu.VMEM((GROUPS, n_dp, chunk, C), f32),
            pltpu.VMEM((TAPS, chunk, C), bf16),
            dma((4,)),
            dma((2, 3)),
            dma((2, 3)),
            dma((GROUPS, n_space)),
            dma((GROUPS, n_space)),
            dma((GROUPS, GT)),
            dma((GROUPS, n_dp)),
            dma((GROUPS, n_dp)),
            dma((TAPS,)),
            dma((GROUPS, n_space)),
            dma((GROUPS, n_space)),
            dma((2,)),
            dma((GROUPS,)),
        ],
        compiler_params=pltpu.CompilerParams(
            vmem_limit_bytes=61 * 2**20, collective_id=0, has_side_effects=True
        ),
        name="sparse_conv",
    )(features[0], jnp.transpose(neighbours, (1, 0, 2)), weight, grad_out[0])
    norm = 1.0 / math.sqrt(n_dp * n_space * voxels)
    return conv[None], gin[None], gw.astype(f32) * norm


def solution(mesh):
    in_specs = (P("dp", "space", None), P("dp", None, "space"), P(), P("dp", "space", None))
    out_specs = (P("dp", "space", None), P("dp", "space", None), P())
    return jax.shard_map(local, mesh=mesh, in_specs=in_specs, out_specs=out_specs, check_vma=False)
```

```python
import functools
import math

import jax
import jax.numpy as jnp
from jax import lax
from jax.experimental import pallas as pl
from jax.experimental.pallas import tpu as pltpu
from jax.sharding import PartitionSpec as P

LAYER, ROW, TAPS, C, TILE = 1024, 16, 27, 128, 128
PAD = ROW
CENTRE = TAPS // 2
AXES, SIDE = 3, 4
ORDER = tuple(range(9, 18)) + tuple(range(0, 9)) + tuple(range(18, 27))
SETS = (((0, 3), (3, 3), (6, 3)), ((9, 6), (15, 6), (21, 6)))
GROUPS = len(SETS)
bf16, f32 = jnp.bfloat16, jnp.float32
MESH = pl.DeviceIdType.MESH


def shift(k):
    return k // 9 - 1, k % 9 // 3 - 1


def one_hot(targets, first):
    local = jnp.where(targets >= 0, targets - first, -1)
    local = jnp.where((local >= 0) & (local < TILE), local, -1)
    local = local.astype(f32).astype(bf16)
    rows = lax.broadcasted_iota(jnp.int32, (TILE, TILE), 0).astype(f32).astype(bf16)
    return jnp.where(
        jnp.broadcast_to(local, (TILE, TILE)) == rows, jnp.ones((), bf16), jnp.zeros((), bf16)
    )


def scatter_tile(feats, grads, targets, first_target, row, taps, picked_f, picked_g):
    hot = [
        one_hot(targets[i], first_target + shift(k)[1] * ROW) for i, k in enumerate(taps)
    ]
    out = jnp.dot(
        jnp.concatenate(hot, 0),
        jnp.concatenate([feats, grads], 1),
        preferred_element_type=f32,
    ).astype(bf16)
    for i, k in enumerate(taps):
        at = pl.ds(pl.multiple_of(row + shift(k)[1] * ROW, ROW), TILE)
        picked_f[at, k * C : (k + 1) * C] = out[i * TILE : (i + 1) * TILE, :C]
        picked_g[at, k * C : (k + 1) * C] = out[i * TILE : (i + 1) * TILE, C:]


def kernel(
    f_hbm, n_hbm, w_hbm, g_hbm,
    conv_hbm, gin_hbm, gw_hbm,
    f_ref, g_ref, n_ref, w_ref, conv_ref, gin_ref, picked_f, picked_g, f_t, g_t,
    n_halo, f_halo, g_halo, part, part_in, first, second, result,
    load_sem, halo_send, halo_recv, a_send, a_recv, b_send, b_recv, c_send, c_recv, d_send, d_recv,
    out_sem, own_sem,
    *, voxels, n_space, unroll, rows,
):
    layers = voxels // LAYER
    tiles, layer_tiles = voxels // TILE, LAYER // TILE
    chunk = C // n_space
    blocks = voxels // rows
    s = lax.axis_index("space")
    q = lax.axis_index("dp")
    base = s * voxels
    x, y, z, core = lax.div(q, SIDE), lax.rem(q, SIDE), lax.div(s, 2), lax.rem(s, 2)
    pos = (z, x, y)

    def on_axis(a, i, c):
        if a == 0:
            return {"dp": q, "space": 2 * i + c}
        return {"dp": SIDE * i + y if a == 1 else SIDE * x + i, "space": 2 * z + c}

    loads = [
        pltpu.make_async_copy(src, dst, load_sem.at[i])
        for i, (src, dst) in enumerate(
            [(n_hbm, n_ref), (f_hbm, f_ref), (g_hbm, g_ref), (w_hbm, w_ref)]
        )
    ]
    for load in loads:
        load.start()

    barrier = pltpu.get_barrier_semaphore()
    pl.semaphore_signal(barrier, inc=1, device_id=on_axis(0, z, 1 - core), device_id_type=MESH)
    for a in range(AXES):
        for d in range(1, SIDE):
            for c in range(2):
                pl.semaphore_signal(
                    barrier, inc=1, device_id=on_axis(a, lax.rem(pos[a] + d, SIDE), c),
                    device_id_type=MESH,
                )
    peers = 1 + AXES * (SIDE - 1) * 2

    for row in (0, ROW, voxels + PAD - ROW, voxels + PAD):
        picked_f[row : row + ROW, :] = jnp.zeros((ROW, TAPS * C), bf16)
        picked_g[row : row + ROW, :] = jnp.zeros((ROW, TAPS * C), bf16)

    def halo_copies(side):
        peer = s + 1 if side == 0 else s - 1
        at = pl.ds(voxels - LAYER if side == 0 else 0, LAYER)
        return [
            pltpu.make_async_remote_copy(
                src_ref=src, dst_ref=dst, send_sem=halo_send.at[side, i],
                recv_sem=halo_recv.at[side, i], device_id={"space": peer}, device_id_type=MESH,
            )
            for i, (src, dst) in enumerate(
                [
                    (n_hbm.at[pl.ds(18 if side == 0 else 0, 9), :, at], n_halo.at[side]),
                    (f_hbm.at[at], f_halo.at[side]),
                    (g_hbm.at[at], g_halo.at[side]),
                ]
            )
        ]

    halos = [halo_copies(0), halo_copies(1)]
    has = [s < n_space - 1, s > 0]

    for side in (0, 1):

        @pl.when(jnp.logical_not(has[1 - side]))
        def _():
            n_halo[side] = jnp.full(n_halo.shape[1:], -1, jnp.int32)
            f_halo[side] = jnp.zeros(f_halo.shape[1:], bf16)
            g_halo[side] = jnp.zeros(g_halo.shape[1:], bf16)

    def each(count, body, unroll=unroll):
        @pl.loop(0, count // unroll)
        def _(i):
            for u in range(unroll):
                body(i * unroll + u)

    def own(t, taps):
        start = pl.multiple_of(t * TILE, TILE)
        at = pl.ds(start, TILE)
        dz = shift(taps[0])[0]
        scatter_tile(
            f_ref[at, :], g_ref[at, :], n_ref[taps[0] : taps[-1] + 1, :, at],
            base + start + dz * LAYER, start + PAD + dz * LAYER, taps, picked_f, picked_g,
        )

    def centre(t):
        start = pl.multiple_of(t * TILE, TILE)
        at, to = pl.ds(start, TILE), pl.ds(start + PAD, TILE)
        lanes = slice(CENTRE * C, (CENTRE + 1) * C)
        feats, grads = f_ref[at, :], g_ref[at, :]
        picked_f[to, lanes] = feats
        picked_g[to, lanes] = grads
        f_t[:, at] = feats.T
        g_t[:, at] = grads.T

    def from_halo(side):
        dz, layer = (1, 0) if side == 0 else (-1, layers - 1)
        taps = range(9 * (dz + 1), 9 * (dz + 1) + 9)

        @pl.when(has[1 - side])
        def _():
            for copy in halos[side]:
                copy.wait_recv()

        def body(t):
            start = pl.multiple_of(t * TILE, TILE)
            at = pl.ds(start, TILE)
            scatter_tile(
                f_halo[side, at, :], g_halo[side, at, :], n_halo[side, :, :, at],
                base + layer * LAYER + start, start + PAD + layer * LAYER, taps,
                picked_f, picked_g,
            )

        each(layer_tiles, body)

    inside = slice(PAD, PAD + voxels)

    def weight_grad(k, count, slot, mirror):
        at = pl.ds(pl.multiple_of(k * C, C), count * C)
        out = jnp.dot(f_t[...], picked_g[inside, at], preferred_element_type=f32)
        for c in range(count):
            part[slot + c] = out[:, c * C : (c + 1) * C].astype(bf16)
        if mirror is not None:
            out = jnp.dot(g_t[...], picked_f[inside, at], preferred_element_type=f32)
            for c in range(count):
                part[mirror - c] = out[:, c * C : (c + 1) * C].T.astype(bf16)

    line = [2 * p + core for p in pos]

    def taps_of(g, a):
        return pl.ds(*SETS[g][a])

    def ring(i, n):
        return lax.rem(i, n)

    def rows_of(i):
        return pl.ds(pl.multiple_of(i * chunk, chunk), chunk)

    def on_line(a, i):
        return on_axis(a, lax.div(i, 2), lax.rem(i, 2))

    def a_copy(g, a, d):
        to = ring(line[a] + d, n_space)
        return pltpu.make_async_remote_copy(
            src_ref=part.at[taps_of(g, a), rows_of(to)], dst_ref=part_in.at[d, taps_of(g, a)],
            send_sem=a_send.at[g, a, d], recv_sem=a_recv.at[g, a, d],
            device_id=on_line(a, to), device_id_type=MESH,
        )

    def axis_copy(held, send, recv, g, a, b, d):
        here = held.at[pos[b], taps_of(g, a)]
        return pltpu.make_async_remote_copy(
            src_ref=here, dst_ref=here, send_sem=send.at[g, a, d], recv_sem=recv.at[g, a, d],
            device_id=on_axis(b, ring(pos[b] + d, SIDE), core), device_id_type=MESH,
        )

    def b_copy(g, a, d):
        return axis_copy(first, b_send, b_recv, g, a, (a + 1) % AXES, d)

    def c_copy(g, a, d):
        return axis_copy(second, c_send, c_recv, g, a, (a + 2) % AXES, d)

    def d_copy(g, a, d):
        return pltpu.make_async_remote_copy(
            src_ref=result.at[taps_of(g, a)], dst_ref=gw_hbm.at[taps_of(g, a), rows_of(line[a])],
            send_sem=d_send.at[g, a, d], recv_sem=d_recv.at[g, a, d],
            device_id=on_line(a, ring(line[a] + d, n_space)), device_id_type=MESH,
        )

    def own_rows(g, a):
        return pltpu.make_async_copy(
            result.at[taps_of(g, a)], gw_hbm.at[taps_of(g, a), rows_of(line[a])], own_sem.at[g, a]
        )

    def each_tap(g, a, body):
        for i in range(SETS[g][a][1]):
            body(SETS[g][a][0] + i)

    def stage_a(g):
        for d in range(1, n_space):
            for a in range(AXES):
                a_copy(g, a, d).start()

    def stage_b(g):
        for a in range(AXES):
            for d in range(1, n_space):
                a_copy(g, a, d).wait_recv()

            def add(k):
                total = part[k, rows_of(line[a]), :].astype(f32)
                for d in range(1, n_space):
                    total = total + part_in[d, k].astype(f32)
                first[pos[(a + 1) % AXES], k] = total.astype(bf16)

            each_tap(g, a, add)
            for d in range(1, SIDE):
                b_copy(g, a, d).start()

    def added(held, k):
        total = held[0, k].astype(f32)
        for i in range(1, SIDE):
            total = total + held[i, k].astype(f32)
        return total.astype(bf16)

    def stage_c(g):
        for a in range(AXES):
            for d in range(1, SIDE):
                b_copy(g, a, d).wait_recv()

            def add(k):
                second[pos[(a + 2) % AXES], k] = added(first, k)

            each_tap(g, a, add)
            for d in range(1, SIDE):
                c_copy(g, a, d).start()

    def stage_d(g):
        for a in range(AXES):
            for d in range(1, SIDE):
                c_copy(g, a, d).wait_recv()

            def add(k):
                result[k] = added(second, k)

            each_tap(g, a, add)
            for d in range(1, n_space):
                d_copy(g, a, d).start()
            own_rows(g, a).start()

    def finish(g):
        for a in range(AXES):
            for d in range(1, n_space):
                d_copy(g, a, d).wait_recv()
            own_rows(g, a).wait()
            for d in range(1, n_space):
                a_copy(g, a, d).wait_send()
                d_copy(g, a, d).wait_send()
            for d in range(1, SIDE):
                b_copy(g, a, d).wait_send()
                c_copy(g, a, d).wait_send()

    pl.semaphore_wait(barrier, peers)
    for side in (1, 0):

        @pl.when(has[side])
        def _():
            for copy in halos[side]:
                copy.start()

    for load in loads[:3]:
        load.wait()

    def first_taps(t):
        centre(t)
        own(t, range(9, 13))

    each(tiles, first_taps)

    @pl.loop(0, 2)
    def _(i):
        weight_grad(9 + 2 * i, 2, 2 * i, 8 - 2 * i)

    weight_grad(CENTRE, 1, 4, None)
    stage_a(0)
    each(tiles - layer_tiles, lambda t: own(t + layer_tiles, range(0, 9)))
    each(tiles, lambda t: own(t, range(14, 18)))
    stage_b(0)
    from_halo(1)

    @pl.loop(0, 4)
    def _(i):
        weight_grad(2 * i, 2, 9 + 2 * i, 26 - 2 * i)

    weight_grad(8, 1, 17, 18)
    stage_a(1)
    stage_c(0)
    each(tiles - layer_tiles, lambda t: own(t, range(18, 27)))
    from_halo(0)
    loads[3].wait()
    stage_b(1)

    def conv(i):
        start = pl.multiple_of(i * rows, rows)
        taps_in = jnp.concatenate([w_ref[TAPS - 1 - k] for k in range(TAPS)], 0)
        conv_ref[pl.ds(start, rows), :] = jnp.dot(
            picked_f[pl.ds(start + PAD, rows), :], taps_in, preferred_element_type=f32
        ).astype(bf16)

    def gin(i):
        start = pl.multiple_of(i * rows, rows)
        taps_out = jnp.concatenate([w_ref[k] for k in range(TAPS)], 1)
        gin_ref[pl.ds(start, rows), :] = lax.dot_general(
            picked_g[pl.ds(start + PAD, rows), :], taps_out, (((1,), (1,)), ((), ())),
            preferred_element_type=f32,
        ).astype(bf16)

    def out_copy(src, dst, which, i):
        at = pl.ds(pl.multiple_of(i * rows, rows), rows)
        return pltpu.make_async_copy(src.at[at], dst.at[at], out_sem.at[which, i])

    @pl.loop(0, blocks)
    def _(i):
        conv(i)
        out_copy(conv_ref, conv_hbm, 0, i).start()

        @pl.when(i == 1)
        def _():
            stage_c(1)

        @pl.when(i == 2)
        def _():
            stage_d(0)

    @pl.loop(0, blocks)
    def _(i):
        gin(i)
        out_copy(gin_ref, gin_hbm, 1, i).start()

        @pl.when(i == 0)
        def _():
            stage_d(1)

    for side in (0, 1):

        @pl.when(has[side])
        def _():
            for copy in halos[side]:
                copy.wait_send()

    for g in range(GROUPS):
        finish(g)
    for i in range(blocks):
        out_copy(conv_ref, conv_hbm, 0, i).wait()
        out_copy(gin_ref, gin_hbm, 1, i).wait()


def finish_kernel(
    conv_in, gin_in, gw_in, conv_out, gin_out, gw_out, conv, gin, raw, scaled, in_sem, out_sem, *, norm
):
    voxels = conv.shape[0]
    pieces = []
    for i in range(0, TAPS, 9):
        taps, out = pl.ds(i, 9), pl.ds(ORDER[i], 9)
        pieces.append((gw_in.at[taps], raw.at[taps], scaled.at[taps], gw_out.at[out]))
    for src, held, dst in ((conv_in, conv, conv_out), (gin_in, gin, gin_out)):
        for i in range(2):
            half = pl.ds(i * (voxels // 2), voxels // 2)
            pieces.append((src.at[half], held.at[half], held.at[half], dst.at[half]))
    ins = [pltpu.make_async_copy(p[0], p[1], in_sem.at[i]) for i, p in enumerate(pieces)]
    outs = [pltpu.make_async_copy(p[2], p[3], out_sem.at[i]) for i, p in enumerate(pieces)]
    for copy in ins:
        copy.start()
    for i in range(len(pieces)):
        ins[i].wait()
        if i < TAPS // 9:
            scaled[9 * i : 9 * i + 9] = raw[9 * i : 9 * i + 9].astype(f32) * norm
        outs[i].start()
    for copy in outs:
        copy.wait()


def local(features, neighbours, weight, grad_out):
    voxels = features.shape[1]
    n_dp, n_space = lax.axis_size("dp"), lax.axis_size("space")
    chunk = C // n_space
    dma = pltpu.SemaphoreType.DMA
    anywhere = pl.BlockSpec(memory_space=pl.ANY)
    conv, gin, gw = pl.pallas_call(
        functools.partial(
            kernel, voxels=voxels, n_space=n_space, unroll=4, rows=1024
        ),
        out_shape=(
            jax.ShapeDtypeStruct((voxels, C), bf16),
            jax.ShapeDtypeStruct((voxels, C), bf16),
            jax.ShapeDtypeStruct((TAPS, C, C), bf16),
        ),
        in_specs=[anywhere] * 4,
        out_specs=(anywhere,) * 3,
        scratch_shapes=[
            pltpu.VMEM((voxels, C), bf16),
            pltpu.VMEM((voxels, C), bf16),
            pltpu.VMEM((TAPS, 1, voxels), jnp.int32),
            pltpu.VMEM((TAPS, C, C), bf16),
            pltpu.VMEM((voxels, C), bf16),
            pltpu.VMEM((voxels, C), bf16),
            pltpu.VMEM((voxels + 2 * PAD, TAPS * C), bf16),
            pltpu.VMEM((voxels + 2 * PAD, TAPS * C), bf16),
            pltpu.VMEM((C, voxels), bf16),
            pltpu.VMEM((C, voxels), bf16),
            pltpu.VMEM((2, 9, 1, LAYER), jnp.int32),
            pltpu.VMEM((2, LAYER, C), bf16),
            pltpu.VMEM((2, LAYER, C), bf16),
            pltpu.VMEM((TAPS, C, C), bf16),
            pltpu.VMEM((n_space, TAPS, chunk, C), bf16),
            pltpu.VMEM((SIDE, TAPS, chunk, C), bf16),
            pltpu.VMEM((SIDE, TAPS, chunk, C), bf16),
            pltpu.VMEM((TAPS, chunk, C), bf16),
            dma((4,)),
            dma((2, 3)),
            dma((2, 3)),
            dma((GROUPS, AXES, n_space)),
            dma((GROUPS, AXES, n_space)),
            dma((GROUPS, AXES, SIDE)),
            dma((GROUPS, AXES, SIDE)),
            dma((GROUPS, AXES, SIDE)),
            dma((GROUPS, AXES, SIDE)),
            dma((GROUPS, AXES, n_space)),
            dma((GROUPS, AXES, n_space)),
            dma((2, voxels // 1024)),
            dma((GROUPS, AXES)),
        ],
        compiler_params=pltpu.CompilerParams(
            vmem_limit_bytes=61 * 2**20, collective_id=0, has_side_effects=True
        ),
        name="sparse_conv",
    )(features[0], jnp.transpose(neighbours, (1, 0, 2)), weight, grad_out[0])
    norm = 1.0 / math.sqrt(n_dp * n_space * voxels)
    conv, gin, gw = pl.pallas_call(
        functools.partial(finish_kernel, norm=norm),
        out_shape=(
            jax.ShapeDtypeStruct((voxels, C), bf16),
            jax.ShapeDtypeStruct((voxels, C), bf16),
            jax.ShapeDtypeStruct((TAPS, C, C), f32),
        ),
        in_specs=[pl.BlockSpec(memory_space=pltpu.HBM)] * 3,
        out_specs=(anywhere,) * 3,
        scratch_shapes=[
            pltpu.VMEM((voxels, C), bf16),
            pltpu.VMEM((voxels, C), bf16),
            pltpu.VMEM((TAPS, C, C), bf16),
            pltpu.VMEM((TAPS, C, C), f32),
            dma((7,)),
            dma((7,)),
        ],
        compiler_params=pltpu.CompilerParams(vmem_limit_bytes=61 * 2**20),
        name="scale",
    )(conv, gin, gw)
    return conv[None], gin[None], gw


def solution(mesh):
    in_specs = (P("dp", "space", None), P("dp", None, "space"), P(), P("dp", "space", None))
    out_specs = (P("dp", "space", None), P("dp", "space", None), P())
    return jax.shard_map(local, mesh=mesh, in_specs=in_specs, out_specs=out_specs, check_vma=False)
```

```python
import functools
import math

import jax
import jax.numpy as jnp
from jax import lax
from jax.experimental import pallas as pl
from jax.experimental.pallas import tpu as pltpu
from jax.sharding import PartitionSpec as P

LAYER, ROW, TAPS, C, TILE = 1024, 16, 27, 128, 128
PAD = ROW
CENTRE = TAPS // 2
AXES, SIDE = 3, 4
ORDER = tuple(range(9, 18)) + tuple(range(0, 9)) + tuple(range(18, 27))
SETS = (((0, 3), (3, 3), (6, 3)), ((9, 6), (15, 6), (21, 6)))
GROUPS = len(SETS)
bf16, f32 = jnp.bfloat16, jnp.float32
MESH = pl.DeviceIdType.MESH


def shift(k):
    return k // 9 - 1, k % 9 // 3 - 1


def one_hot(targets, first):
    local = jnp.where(targets >= 0, targets - first, -1)
    local = jnp.where((local >= 0) & (local < TILE), local, -1)
    local = local.astype(f32).astype(bf16)
    rows = lax.broadcasted_iota(jnp.int32, (TILE, TILE), 0).astype(f32).astype(bf16)
    return jnp.where(
        jnp.broadcast_to(local, (TILE, TILE)) == rows, jnp.ones((), bf16), jnp.zeros((), bf16)
    )


def scatter_tile(feats, grads, targets, first_target, row, taps, picked_f, picked_g):
    hot = [
        one_hot(targets[i], first_target + shift(k)[1] * ROW) for i, k in enumerate(taps)
    ]
    hot = jnp.concatenate(hot, 0)
    out_f = jnp.dot(hot, feats, preferred_element_type=f32).astype(bf16)
    out_g = jnp.dot(hot, grads, preferred_element_type=f32).astype(bf16)
    for i, k in enumerate(taps):
        at = pl.ds(pl.multiple_of(row + shift(k)[1] * ROW, ROW), TILE)
        picked_f[at, k * C : (k + 1) * C] = out_f[i * TILE : (i + 1) * TILE]
        picked_g[at, k * C : (k + 1) * C] = out_g[i * TILE : (i + 1) * TILE]


def kernel(
    f_hbm, n_hbm, w_hbm, g_hbm,
    conv_hbm, gin_hbm, gw_hbm,
    f_ref, g_ref, n_ref, w_ref, conv_ref, gin_ref, picked_f, picked_g, f_t, g_t,
    n_halo, f_halo, g_halo, part, part_in, first, second, result,
    load_sem, halo_send, halo_recv, a_send, a_recv, b_send, b_recv, c_send, c_recv, d_send, d_recv,
    out_sem, own_sem,
    *, voxels, n_space, rows,
):
    layers = voxels // LAYER
    tiles, layer_tiles = voxels // TILE, LAYER // TILE
    chunk = C // n_space
    blocks = voxels // rows
    s = lax.axis_index("space")
    q = lax.axis_index("dp")
    base = s * voxels
    x, y, z, core = lax.div(q, SIDE), lax.rem(q, SIDE), lax.div(s, 2), lax.rem(s, 2)
    pos = (z, x, y)

    def on_axis(a, i, c):
        if a == 0:
            return {"dp": q, "space": 2 * i + c}
        return {"dp": SIDE * i + y if a == 1 else SIDE * x + i, "space": 2 * z + c}

    loads = [
        pltpu.make_async_copy(src, dst, load_sem.at[i])
        for i, (src, dst) in enumerate(
            [(n_hbm, n_ref), (f_hbm, f_ref), (g_hbm, g_ref), (w_hbm, w_ref)]
        )
    ]
    for load in loads:
        load.start()

    barrier = pltpu.get_barrier_semaphore()
    pl.semaphore_signal(barrier, inc=1, device_id=on_axis(0, z, 1 - core), device_id_type=MESH)
    for a in range(AXES):
        for d in range(1, SIDE):
            for c in range(2):
                pl.semaphore_signal(
                    barrier, inc=1, device_id=on_axis(a, lax.rem(pos[a] + d, SIDE), c),
                    device_id_type=MESH,
                )
    peers = 1 + AXES * (SIDE - 1) * 2

    for row in (0, ROW, voxels + PAD - ROW, voxels + PAD):
        picked_f[row : row + ROW, :] = jnp.zeros((ROW, TAPS * C), bf16)
        picked_g[row : row + ROW, :] = jnp.zeros((ROW, TAPS * C), bf16)

    def halo_copies(side):
        peer = s + 1 if side == 0 else s - 1
        at = pl.ds(voxels - LAYER if side == 0 else 0, LAYER)
        return [
            pltpu.make_async_remote_copy(
                src_ref=src, dst_ref=dst, send_sem=halo_send.at[side, i],
                recv_sem=halo_recv.at[side, i], device_id={"space": peer}, device_id_type=MESH,
            )
            for i, (src, dst) in enumerate(
                [
                    (n_hbm.at[pl.ds(18 if side == 0 else 0, 9), :, at], n_halo.at[side]),
                    (f_hbm.at[at], f_halo.at[side]),
                    (g_hbm.at[at], g_halo.at[side]),
                ]
            )
        ]

    halos = [halo_copies(0), halo_copies(1)]
    has = [s < n_space - 1, s > 0]

    for side in (0, 1):

        @pl.when(jnp.logical_not(has[1 - side]))
        def _():
            n_halo[side] = jnp.full(n_halo.shape[1:], -1, jnp.int32)
            f_halo[side] = jnp.zeros(f_halo.shape[1:], bf16)
            g_halo[side] = jnp.zeros(g_halo.shape[1:], bf16)

    def each(count, body):
        for t in range(count):
            body(t)

    def own(t, taps):
        start = t * TILE
        at = pl.ds(start, TILE)
        dz = shift(taps[0])[0]
        scatter_tile(
            f_ref[at, :], g_ref[at, :], n_ref[taps[0] : taps[-1] + 1, :, at],
            base + start + dz * LAYER, start + PAD + dz * LAYER, taps, picked_f, picked_g,
        )

    def centre(t):
        start = t * TILE
        at, to = pl.ds(start, TILE), pl.ds(start + PAD, TILE)
        lanes = slice(CENTRE * C, (CENTRE + 1) * C)
        feats, grads = f_ref[at, :], g_ref[at, :]
        picked_f[to, lanes] = feats
        picked_g[to, lanes] = grads
        f_t[:, at] = feats.T
        g_t[:, at] = grads.T

    def from_halo(side):
        dz, layer = (1, 0) if side == 0 else (-1, layers - 1)
        taps = range(9 * (dz + 1), 9 * (dz + 1) + 9)

        @pl.when(has[1 - side])
        def _():
            for copy in halos[side]:
                copy.wait_recv()

        def body(t):
            start = t * TILE
            at = pl.ds(start, TILE)
            scatter_tile(
                f_halo[side, at, :], g_halo[side, at, :], n_halo[side, :, :, at],
                base + layer * LAYER + start, start + PAD + layer * LAYER, taps,
                picked_f, picked_g,
            )

        each(layer_tiles, body)

    inside = slice(PAD, PAD + voxels)

    def weight_grad(k, count, slot, mirror):
        at = slice(k * C, (k + count) * C)
        out = jnp.dot(f_t[...], picked_g[inside, at], preferred_element_type=f32)
        for c in range(count):
            part[slot + c] = out[:, c * C : (c + 1) * C].astype(bf16)
        if mirror is not None:
            out = jnp.dot(g_t[...], picked_f[inside, at], preferred_element_type=f32)
            for c in range(count):
                part[mirror - c] = out[:, c * C : (c + 1) * C].T.astype(bf16)

    line = [2 * p + core for p in pos]

    def taps_of(g, a):
        return pl.ds(*SETS[g][a])

    def ring(i, n):
        return lax.rem(i, n)

    def rows_of(i):
        return pl.ds(pl.multiple_of(i * chunk, chunk), chunk)

    def on_line(a, i):
        return on_axis(a, lax.div(i, 2), lax.rem(i, 2))

    def a_copy(g, a, d):
        to = ring(line[a] + d, n_space)
        return pltpu.make_async_remote_copy(
            src_ref=part.at[taps_of(g, a), rows_of(to)], dst_ref=part_in.at[d, taps_of(g, a)],
            send_sem=a_send.at[g, a, d], recv_sem=a_recv.at[g, a, d],
            device_id=on_line(a, to), device_id_type=MESH,
        )

    def axis_copy(held, send, recv, g, a, b, d):
        here = held.at[pos[b], taps_of(g, a)]
        return pltpu.make_async_remote_copy(
            src_ref=here, dst_ref=here, send_sem=send.at[g, a, d], recv_sem=recv.at[g, a, d],
            device_id=on_axis(b, ring(pos[b] + d, SIDE), core), device_id_type=MESH,
        )

    def b_copy(g, a, d):
        return axis_copy(first, b_send, b_recv, g, a, (a + 1) % AXES, d)

    def c_copy(g, a, d):
        return axis_copy(second, c_send, c_recv, g, a, (a + 2) % AXES, d)

    def d_copy(g, a, d):
        return pltpu.make_async_remote_copy(
            src_ref=result.at[taps_of(g, a)], dst_ref=gw_hbm.at[taps_of(g, a), rows_of(line[a])],
            send_sem=d_send.at[g, a, d], recv_sem=d_recv.at[g, a, d],
            device_id=on_line(a, ring(line[a] + d, n_space)), device_id_type=MESH,
        )

    def own_rows(g, a):
        return pltpu.make_async_copy(
            result.at[taps_of(g, a)], gw_hbm.at[taps_of(g, a), rows_of(line[a])], own_sem.at[g, a]
        )

    def each_tap(g, a, body):
        for i in range(SETS[g][a][1]):
            body(SETS[g][a][0] + i)

    def stage_a(g):
        for d in range(1, n_space):
            for a in range(AXES):
                a_copy(g, a, d).start()

    def stage_b(g):
        for a in range(AXES):
            for d in range(1, n_space):
                a_copy(g, a, d).wait_recv()

            def add(k):
                total = part[k, rows_of(line[a]), :].astype(f32)
                for d in range(1, n_space):
                    total = total + part_in[d, k].astype(f32)
                first[pos[(a + 1) % AXES], k] = total.astype(bf16)

            each_tap(g, a, add)
            for d in range(1, SIDE):
                b_copy(g, a, d).start()

    def added(held, k):
        total = held[0, k].astype(f32)
        for i in range(1, SIDE):
            total = total + held[i, k].astype(f32)
        return total.astype(bf16)

    def stage_c(g):
        for a in range(AXES):
            for d in range(1, SIDE):
                b_copy(g, a, d).wait_recv()

            def add(k):
                second[pos[(a + 2) % AXES], k] = added(first, k)

            each_tap(g, a, add)
            for d in range(1, SIDE):
                c_copy(g, a, d).start()

    def stage_d(g):
        for a in range(AXES):
            for d in range(1, SIDE):
                c_copy(g, a, d).wait_recv()

            def add(k):
                result[k] = added(second, k)

            each_tap(g, a, add)
            for d in range(1, n_space):
                d_copy(g, a, d).start()
            own_rows(g, a).start()

    def finish(g):
        for a in range(AXES):
            for d in range(1, n_space):
                d_copy(g, a, d).wait_recv()
            own_rows(g, a).wait()
            for d in range(1, n_space):
                a_copy(g, a, d).wait_send()
                d_copy(g, a, d).wait_send()
            for d in range(1, SIDE):
                b_copy(g, a, d).wait_send()
                c_copy(g, a, d).wait_send()

    pl.semaphore_wait(barrier, peers)
    for side in (1, 0):

        @pl.when(has[side])
        def _():
            for copy in halos[side]:
                copy.start()

    for load in loads[:3]:
        load.wait()

    def first_taps(t):
        centre(t)
        own(t, range(9, 13))

    each(tiles, first_taps)

    weight_grad(9, 4, 0, 8)
    weight_grad(CENTRE, 1, 4, None)
    stage_a(0)
    each(tiles - layer_tiles, lambda t: own(t + layer_tiles, range(0, 9)))
    each(tiles, lambda t: own(t, range(14, 18)))
    stage_b(0)
    from_halo(1)

    weight_grad(0, 4, 9, 26)
    weight_grad(4, 4, 13, 22)
    weight_grad(8, 1, 17, 18)
    stage_a(1)
    stage_c(0)
    each(tiles - layer_tiles, lambda t: own(t, range(18, 27)))
    from_halo(0)
    loads[3].wait()
    stage_b(1)

    def conv(i):
        start = pl.multiple_of(i * rows, rows)
        taps_in = jnp.concatenate([w_ref[TAPS - 1 - k] for k in range(TAPS)], 0)
        conv_ref[pl.ds(start, rows), :] = jnp.dot(
            picked_f[pl.ds(start + PAD, rows), :], taps_in, preferred_element_type=f32
        ).astype(bf16)

    def gin(i):
        start = pl.multiple_of(i * rows, rows)
        taps_out = jnp.concatenate([w_ref[k] for k in range(TAPS)], 1)
        gin_ref[pl.ds(start, rows), :] = lax.dot_general(
            picked_g[pl.ds(start + PAD, rows), :], taps_out, (((1,), (1,)), ((), ())),
            preferred_element_type=f32,
        ).astype(bf16)

    def out_copy(src, dst, which, i):
        at = pl.ds(pl.multiple_of(i * rows, rows), rows)
        return pltpu.make_async_copy(src.at[at], dst.at[at], out_sem.at[which, i])

    @pl.loop(0, blocks)
    def _(i):
        conv(i)
        out_copy(conv_ref, conv_hbm, 0, i).start()

        @pl.when(i == 1)
        def _():
            stage_c(1)

        @pl.when(i == 2)
        def _():
            stage_d(0)

    @pl.loop(0, blocks)
    def _(i):
        gin(i)
        out_copy(gin_ref, gin_hbm, 1, i).start()

        @pl.when(i == 0)
        def _():
            stage_d(1)

    for side in (0, 1):

        @pl.when(has[side])
        def _():
            for copy in halos[side]:
                copy.wait_send()

    for g in range(GROUPS):
        finish(g)
    for i in range(blocks):
        out_copy(conv_ref, conv_hbm, 0, i).wait()
        out_copy(gin_ref, gin_hbm, 1, i).wait()


def finish_kernel(
    conv_in, gin_in, gw_in, conv_out, gin_out, gw_out, conv, gin, raw, scaled, in_sem, out_sem, *, norm
):
    voxels = conv.shape[0]
    pieces = []
    for i in range(0, TAPS, 9):
        taps, out = pl.ds(i, 9), pl.ds(ORDER[i], 9)
        pieces.append((gw_in.at[taps], raw.at[taps], scaled.at[taps], gw_out.at[out]))
    for src, held, dst in ((conv_in, conv, conv_out), (gin_in, gin, gin_out)):
        for i in range(2):
            half = pl.ds(i * (voxels // 2), voxels // 2)
            pieces.append((src.at[half], held.at[half], held.at[half], dst.at[half]))
    ins = [pltpu.make_async_copy(p[0], p[1], in_sem.at[i]) for i, p in enumerate(pieces)]
    outs = [pltpu.make_async_copy(p[2], p[3], out_sem.at[i]) for i, p in enumerate(pieces)]
    for copy in ins:
        copy.start()
    for i in range(len(pieces)):
        ins[i].wait()
        if i < TAPS // 9:
            scaled[9 * i : 9 * i + 9] = raw[9 * i : 9 * i + 9].astype(f32) * norm
        outs[i].start()
    for copy in outs:
        copy.wait()


def local(features, neighbours, weight, grad_out):
    voxels = features.shape[1]
    n_dp, n_space = lax.axis_size("dp"), lax.axis_size("space")
    chunk = C // n_space
    dma = pltpu.SemaphoreType.DMA
    anywhere = pl.BlockSpec(memory_space=pl.ANY)
    conv, gin, gw = pl.pallas_call(
        functools.partial(
            kernel, voxels=voxels, n_space=n_space, rows=1024
        ),
        out_shape=(
            jax.ShapeDtypeStruct((voxels, C), bf16),
            jax.ShapeDtypeStruct((voxels, C), bf16),
            jax.ShapeDtypeStruct((TAPS, C, C), bf16),
        ),
        in_specs=[anywhere] * 4,
        out_specs=(anywhere,) * 3,
        scratch_shapes=[
            pltpu.VMEM((voxels, C), bf16),
            pltpu.VMEM((voxels, C), bf16),
            pltpu.VMEM((TAPS, 1, voxels), jnp.int32),
            pltpu.VMEM((TAPS, C, C), bf16),
            pltpu.VMEM((voxels, C), bf16),
            pltpu.VMEM((voxels, C), bf16),
            pltpu.VMEM((voxels + 2 * PAD, TAPS * C), bf16),
            pltpu.VMEM((voxels + 2 * PAD, TAPS * C), bf16),
            pltpu.VMEM((C, voxels), bf16),
            pltpu.VMEM((C, voxels), bf16),
            pltpu.VMEM((2, 9, 1, LAYER), jnp.int32),
            pltpu.VMEM((2, LAYER, C), bf16),
            pltpu.VMEM((2, LAYER, C), bf16),
            pltpu.VMEM((TAPS, C, C), bf16),
            pltpu.VMEM((n_space, TAPS, chunk, C), bf16),
            pltpu.VMEM((SIDE, TAPS, chunk, C), bf16),
            pltpu.VMEM((SIDE, TAPS, chunk, C), bf16),
            pltpu.VMEM((TAPS, chunk, C), bf16),
            dma((4,)),
            dma((2, 3)),
            dma((2, 3)),
            dma((GROUPS, AXES, n_space)),
            dma((GROUPS, AXES, n_space)),
            dma((GROUPS, AXES, SIDE)),
            dma((GROUPS, AXES, SIDE)),
            dma((GROUPS, AXES, SIDE)),
            dma((GROUPS, AXES, SIDE)),
            dma((GROUPS, AXES, n_space)),
            dma((GROUPS, AXES, n_space)),
            dma((2, voxels // 1024)),
            dma((GROUPS, AXES)),
        ],
        compiler_params=pltpu.CompilerParams(
            vmem_limit_bytes=61 * 2**20, collective_id=0, has_side_effects=True
        ),
        name="sparse_conv",
    )(features[0], jnp.transpose(neighbours, (1, 0, 2)), weight, grad_out[0])
    norm = 1.0 / math.sqrt(n_dp * n_space * voxels)
    conv, gin, gw = pl.pallas_call(
        functools.partial(finish_kernel, norm=norm),
        out_shape=(
            jax.ShapeDtypeStruct((voxels, C), bf16),
            jax.ShapeDtypeStruct((voxels, C), bf16),
            jax.ShapeDtypeStruct((TAPS, C, C), f32),
        ),
        in_specs=[pl.BlockSpec(memory_space=pltpu.HBM)] * 3,
        out_specs=(anywhere,) * 3,
        scratch_shapes=[
            pltpu.VMEM((voxels, C), bf16),
            pltpu.VMEM((voxels, C), bf16),
            pltpu.VMEM((TAPS, C, C), bf16),
            pltpu.VMEM((TAPS, C, C), f32),
            dma((7,)),
            dma((7,)),
        ],
        compiler_params=pltpu.CompilerParams(vmem_limit_bytes=61 * 2**20),
        name="scale",
    )(conv, gin, gw)
    return conv[None], gin[None], gw


def solution(mesh):
    in_specs = (P("dp", "space", None), P("dp", None, "space"), P(), P("dp", "space", None))
    out_specs = (P("dp", "space", None), P("dp", "space", None), P())
    return jax.shard_map(local, mesh=mesh, in_specs=in_specs, out_specs=out_specs, check_vma=False)
```

```python
import functools
import math

import jax
import jax.numpy as jnp
from jax import lax
from jax.experimental import pallas as pl
from jax.experimental.pallas import tpu as pltpu
from jax.sharding import PartitionSpec as P

LAYER, ROW, TAPS, C, TILE = 1024, 16, 27, 128, 128
PAD = ROW
CENTRE = TAPS // 2
AXES, SIDE = 3, 4
ORDER = tuple(range(9, 18)) + tuple(range(0, 9)) + tuple(range(18, 27))
SETS = ({1: (0, 9)}, {0: (9, 6), 1: (15, 6), 2: (21, 6)})
GROUPS = len(SETS)
bf16, f32 = jnp.bfloat16, jnp.float32
MESH = pl.DeviceIdType.MESH


def shift(k):
    return k // 9 - 1, k % 9 // 3 - 1


def one_hot(targets, first):
    local = jnp.where(targets >= 0, targets - first, -1)
    local = jnp.where((local >= 0) & (local < TILE), local, -1)
    local = local.astype(f32).astype(bf16)
    rows = lax.broadcasted_iota(jnp.int32, (TILE, TILE), 0).astype(f32).astype(bf16)
    return jnp.where(
        jnp.broadcast_to(local, (TILE, TILE)) == rows, jnp.ones((), bf16), jnp.zeros((), bf16)
    )


def scatter_tile(feats, grads, targets, first_target, row, taps, picked_f, picked_g):
    hot = [
        one_hot(targets[i], first_target + shift(k)[1] * ROW) for i, k in enumerate(taps)
    ]
    hot = jnp.concatenate(hot, 0)
    out_f = jnp.dot(hot, feats, preferred_element_type=f32).astype(bf16)
    out_g = jnp.dot(hot, grads, preferred_element_type=f32).astype(bf16)
    for i, k in enumerate(taps):
        at = pl.ds(pl.multiple_of(row + shift(k)[1] * ROW, ROW), TILE)
        picked_f[at, k * C : (k + 1) * C] = out_f[i * TILE : (i + 1) * TILE]
        picked_g[at, k * C : (k + 1) * C] = out_g[i * TILE : (i + 1) * TILE]


def kernel(
    f_hbm, n_hbm, w_hbm, g_hbm,
    conv_hbm, gin_hbm, gw_hbm,
    f_ref, g_ref, n_ref, w_ref, conv_ref, gin_ref, picked_f, picked_g, f_t, g_t,
    held, n_halo, f_halo, g_halo, part, part_in, first, second, result,
    load_sem, halo_send, halo_recv, a_send, a_recv, b_send, b_recv, c_send, c_recv, d_send, d_recv,
    out_sem, own_sem,
    *, voxels, n_space, rows,
):
    layers = voxels // LAYER
    tiles, layer_tiles = voxels // TILE, LAYER // TILE
    chunk = C // n_space
    blocks = voxels // rows
    s = lax.axis_index("space")
    q = lax.axis_index("dp")
    base = s * voxels
    x, y, z, core = lax.div(q, SIDE), lax.rem(q, SIDE), lax.div(s, 2), lax.rem(s, 2)
    pos = (z, x, y)

    def on_axis(a, i, c):
        if a == 0:
            return {"dp": q, "space": 2 * i + c}
        return {"dp": SIDE * i + y if a == 1 else SIDE * x + i, "space": 2 * z + c}

    loads = [
        pltpu.make_async_copy(src, dst, load_sem.at[i])
        for i, (src, dst) in enumerate(
            [(n_hbm, n_ref), (f_hbm, f_ref), (g_hbm, g_ref), (w_hbm, w_ref)]
        )
    ]
    for load in loads:
        load.start()

    barrier = pltpu.get_barrier_semaphore()
    pl.semaphore_signal(barrier, inc=1, device_id=on_axis(0, z, 1 - core), device_id_type=MESH)
    for a in range(AXES):
        for d in range(1, SIDE):
            for c in range(2):
                pl.semaphore_signal(
                    barrier, inc=1, device_id=on_axis(a, lax.rem(pos[a] + d, SIDE), c),
                    device_id_type=MESH,
                )
    peers = 1 + AXES * (SIDE - 1) * 2

    for row in (0, ROW, voxels + PAD - LAYER - ROW, voxels + PAD - ROW, voxels + PAD):
        picked_f[row : row + ROW, :] = jnp.zeros((ROW, TAPS * C), bf16)
        picked_g[row : row + ROW, :] = jnp.zeros((ROW, TAPS * C), bf16)

    def halo_copies(side):
        peer = s + 1 if side == 0 else s - 1
        at = pl.ds(voxels - LAYER if side == 0 else 0, LAYER)
        return [
            pltpu.make_async_remote_copy(
                src_ref=src, dst_ref=dst, send_sem=halo_send.at[side, i],
                recv_sem=halo_recv.at[side, i], device_id={"space": peer}, device_id_type=MESH,
            )
            for i, (src, dst) in enumerate(
                [
                    (n_hbm.at[pl.ds(18 if side == 0 else 0, 9), :, at], n_halo.at[side]),
                    (f_hbm.at[at], f_halo.at[side]),
                    (g_hbm.at[at], g_halo.at[side]),
                ]
            )
        ]

    halos = [halo_copies(0), halo_copies(1)]
    has = [s < n_space - 1, s > 0]

    for side in (0, 1):

        @pl.when(jnp.logical_not(has[1 - side]))
        def _():
            n_halo[side] = jnp.full(n_halo.shape[1:], -1, jnp.int32)
            f_halo[side] = jnp.zeros(f_halo.shape[1:], bf16)
            g_halo[side] = jnp.zeros(g_halo.shape[1:], bf16)

    def each(count, body):
        for t in range(count):
            body(t)

    def own(t, taps):
        start = t * TILE
        at = pl.ds(start, TILE)
        dz = shift(taps[0])[0]
        scatter_tile(
            f_ref[at, :], g_ref[at, :], n_ref[taps[0] : taps[-1] + 1, :, at],
            base + start + dz * LAYER, start + PAD + dz * LAYER, taps, picked_f, picked_g,
        )

    def centre(t):
        start = t * TILE
        at, to = pl.ds(start, TILE), pl.ds(start + PAD, TILE)
        lanes = slice(CENTRE * C, (CENTRE + 1) * C)
        feats, grads = f_ref[at, :], g_ref[at, :]
        picked_f[to, lanes] = feats
        picked_g[to, lanes] = grads
        f_t[:, at] = feats.T
        g_t[:, at] = grads.T

    def from_halo(side):
        dz, layer = (1, 0) if side == 0 else (-1, layers - 1)
        taps = range(9 * (dz + 1), 9 * (dz + 1) + 9)

        @pl.when(has[1 - side])
        def _():
            for copy in halos[side]:
                copy.wait_recv()

        def body(t):
            start = t * TILE
            at = pl.ds(start, TILE)
            scatter_tile(
                f_halo[side, at, :], g_halo[side, at, :], n_halo[side, :, :, at],
                base + layer * LAYER + start, start + PAD + layer * LAYER, taps,
                picked_f, picked_g,
            )

        each(layer_tiles, body)

    near = voxels - LAYER

    def products(k, count, begin, end):
        at, rows_in, here = slice(k * C, (k + count) * C), slice(PAD + begin, PAD + end), slice(begin, end)
        return (
            jnp.dot(f_t[:, here], picked_g[rows_in, at], preferred_element_type=f32),
            jnp.dot(g_t[:, here], picked_f[rows_in, at], preferred_element_type=f32),
        )

    def put(k, count, straight, mirrored):
        for c in range(count):
            lanes = slice(c * C, (c + 1) * C)
            part[ORDER.index(k + c)] = straight[:, lanes].astype(bf16)
            if mirrored is not None:
                part[ORDER.index(TAPS - 1 - k - c)] = mirrored[:, lanes].T.astype(bf16)

    parts_below = ((0, 4), (4, 4), (8, 1))

    def weight_grad_same():
        put(9, 4, *products(9, 4, 0, voxels))
        put(CENTRE, 1, jnp.dot(f_t[...], g_ref[...], preferred_element_type=f32), None)

    def weight_grad_near():
        for k, count in parts_below:
            lanes = slice(k * C, (k + count) * C)
            held[0, :, lanes], held[1, :, lanes] = products(k, count, 0, near)

    def weight_grad_far():
        for k, count in parts_below:
            lanes = slice(k * C, (k + count) * C)
            straight, mirrored = products(k, count, near, voxels)
            put(k, count, held[0, :, lanes] + straight, held[1, :, lanes] + mirrored)

    line = [2 * p + core for p in pos]

    def taps_of(g, a):
        return pl.ds(*SETS[g][a])

    def ring(i, n):
        return lax.rem(i, n)

    def rows_of(i):
        return pl.ds(pl.multiple_of(i * chunk, chunk), chunk)

    def on_line(a, i):
        return on_axis(a, lax.div(i, 2), lax.rem(i, 2))

    def a_copy(g, a, d):
        to = ring(line[a] + d, n_space)
        return pltpu.make_async_remote_copy(
            src_ref=part.at[taps_of(g, a), rows_of(to)], dst_ref=part_in.at[d, taps_of(g, a)],
            send_sem=a_send.at[g], recv_sem=a_recv.at[g],
            device_id=on_line(a, to), device_id_type=MESH,
        )

    def axis_copy(values, send, recv, g, a, b, d):
        here = values.at[pos[b], taps_of(g, a)]
        return pltpu.make_async_remote_copy(
            src_ref=here, dst_ref=here, send_sem=send.at[g], recv_sem=recv.at[g],
            device_id=on_axis(b, ring(pos[b] + d, SIDE), core), device_id_type=MESH,
        )

    def b_copy(g, a, d):
        return axis_copy(first, b_send, b_recv, g, a, (a + 1) % AXES, d)

    def c_copy(g, a, d):
        return axis_copy(second, c_send, c_recv, g, a, (a + 2) % AXES, d)

    def d_copy(g, a, d):
        return pltpu.make_async_remote_copy(
            src_ref=result.at[taps_of(g, a)], dst_ref=gw_hbm.at[taps_of(g, a), rows_of(line[a])],
            send_sem=d_send.at[g], recv_sem=d_recv.at[g],
            device_id=on_line(a, ring(line[a] + d, n_space)), device_id_type=MESH,
        )

    def own_rows(g, a):
        return pltpu.make_async_copy(
            result.at[taps_of(g, a)], gw_hbm.at[taps_of(g, a), rows_of(line[a])], own_sem.at[g, a]
        )

    def wait_all(values, g, sem):
        start = min(at for at, _ in SETS[g].values())
        count = sum(n for _, n in SETS[g].values())
        held_by = values.at[pl.ds(1, values.shape[0] - 1), pl.ds(start, count)]
        pltpu.make_async_copy(held_by, held_by, sem.at[g]).wait()

    def each_tap(g, a, body):
        for i in range(SETS[g][a][1]):
            body(SETS[g][a][0] + i)

    def stage_a(g):
        for d in range(1, n_space):
            for a in SETS[g]:
                a_copy(g, a, d).start()

    def stage_b(g):
        wait_all(part_in, g, a_recv)
        for a in SETS[g]:

            def add(k):
                total = part[k, rows_of(line[a]), :].astype(f32)
                for d in range(1, n_space):
                    total = total + part_in[d, k].astype(f32)
                first[pos[(a + 1) % AXES], k] = total.astype(bf16)

            each_tap(g, a, add)
            for d in range(1, SIDE):
                b_copy(g, a, d).start()

    def added(values, k):
        total = values[0, k].astype(f32)
        for i in range(1, SIDE):
            total = total + values[i, k].astype(f32)
        return total.astype(bf16)

    def stage_c(g):
        wait_all(first, g, b_recv)
        for a in SETS[g]:

            def add(k):
                second[pos[(a + 2) % AXES], k] = added(first, k)

            each_tap(g, a, add)
            for d in range(1, SIDE):
                c_copy(g, a, d).start()

    def stage_d(g):
        wait_all(second, g, c_recv)
        for a in SETS[g]:

            def add(k):
                result[k] = added(second, k)

            each_tap(g, a, add)
            for d in range(1, n_space):
                d_copy(g, a, d).start()
            own_rows(g, a).start()

    def sent(g):
        wait_all(part_in, g, a_send)
        wait_all(first, g, b_send)
        wait_all(second, g, c_send)

    def finish(g):
        for a in SETS[g]:
            own_rows(g, a).wait()
        wait_all(part_in, g, d_send)
        wait_all(part_in, g, d_recv)

    pl.semaphore_wait(barrier, peers)
    for side in (1, 0):

        @pl.when(has[side])
        def _():
            for copy in halos[side]:
                copy.start()

    for load in loads[:3]:
        load.wait()

    def first_taps(t):
        centre(t)
        own(t, range(9, 13))

    each(tiles, first_taps)
    weight_grad_same()
    stage_a(0)
    each(tiles - layer_tiles, lambda t: own(t + layer_tiles, range(0, 9)))
    weight_grad_near()
    stage_b(0)
    from_halo(1)
    weight_grad_far()
    stage_a(1)
    each(tiles, lambda t: own(t, range(14, 18)))
    each(tiles - layer_tiles, lambda t: own(t, range(18, 27)))
    stage_b(1)
    stage_c(0)
    from_halo(0)
    loads[3].wait()

    def conv(i):
        start = pl.multiple_of(i * rows, rows)
        taps_in = jnp.concatenate([w_ref[TAPS - 1 - k] for k in range(TAPS)], 0)
        conv_ref[pl.ds(start, rows), :] = jnp.dot(
            picked_f[pl.ds(start + PAD, rows), :], taps_in, preferred_element_type=f32
        ).astype(bf16)

    def gin(i):
        start = pl.multiple_of(i * rows, rows)
        taps_out = jnp.concatenate([w_ref[k] for k in range(TAPS)], 1)
        gin_ref[pl.ds(start, rows), :] = lax.dot_general(
            picked_g[pl.ds(start + PAD, rows), :], taps_out, (((1,), (1,)), ((), ())),
            preferred_element_type=f32,
        ).astype(bf16)

    def out_copy(src, dst, which, i):
        at = pl.ds(pl.multiple_of(i * rows, rows), rows)
        return pltpu.make_async_copy(src.at[at], dst.at[at], out_sem.at[which, i])

    @pl.loop(0, blocks)
    def _(i):
        conv(i)
        out_copy(conv_ref, conv_hbm, 0, i).start()

        @pl.when(i == 1)
        def _():
            stage_c(1)
            stage_d(0)

    @pl.loop(0, blocks)
    def _(i):
        gin(i)
        out_copy(gin_ref, gin_hbm, 1, i).start()

        @pl.when(i == 0)
        def _():
            stage_d(1)

    for side in (0, 1):

        @pl.when(has[side])
        def _():
            for copy in halos[side]:
                copy.wait_send()

    for g in range(GROUPS):
        sent(g)
    for i in range(blocks):
        out_copy(conv_ref, conv_hbm, 0, i).wait()
        out_copy(gin_ref, gin_hbm, 1, i).wait()
    for g in range(GROUPS):
        finish(g)


def finish_kernel(
    conv_in, gin_in, gw_in, conv_out, gin_out, gw_out, conv, gin, raw, scaled, in_sem, out_sem, *, norm
):
    voxels = conv.shape[0]
    pieces = []
    for i in range(0, TAPS, 9):
        taps, out = pl.ds(i, 9), pl.ds(ORDER[i], 9)
        pieces.append((gw_in.at[taps], raw.at[taps], scaled.at[taps], gw_out.at[out]))
    for src, held, dst in ((conv_in, conv, conv_out), (gin_in, gin, gin_out)):
        for i in range(2):
            half = pl.ds(i * (voxels // 2), voxels // 2)
            pieces.append((src.at[half], held.at[half], held.at[half], dst.at[half]))
    ins = [pltpu.make_async_copy(p[0], p[1], in_sem.at[i]) for i, p in enumerate(pieces)]
    outs = [pltpu.make_async_copy(p[2], p[3], out_sem.at[i]) for i, p in enumerate(pieces)]
    for copy in ins:
        copy.start()
    for i in range(len(pieces)):
        ins[i].wait()
        if i < TAPS // 9:
            scaled[9 * i : 9 * i + 9] = raw[9 * i : 9 * i + 9].astype(f32) * norm
        outs[i].start()
    for copy in outs:
        copy.wait()


def local(features, neighbours, weight, grad_out):
    voxels = features.shape[1]
    n_dp, n_space = lax.axis_size("dp"), lax.axis_size("space")
    chunk = C // n_space
    dma = pltpu.SemaphoreType.DMA
    anywhere = pl.BlockSpec(memory_space=pl.ANY)
    conv, gin, gw = pl.pallas_call(
        functools.partial(
            kernel, voxels=voxels, n_space=n_space, rows=1024
        ),
        out_shape=(
            jax.ShapeDtypeStruct((voxels, C), bf16),
            jax.ShapeDtypeStruct((voxels, C), bf16),
            jax.ShapeDtypeStruct((TAPS, C, C), bf16),
        ),
        in_specs=[anywhere] * 4,
        out_specs=(anywhere,) * 3,
        scratch_shapes=[
            pltpu.VMEM((voxels, C), bf16),
            pltpu.VMEM((voxels, C), bf16),
            pltpu.VMEM((TAPS, 1, voxels), jnp.int32),
            pltpu.VMEM((TAPS, C, C), bf16),
            pltpu.VMEM((voxels, C), bf16),
            pltpu.VMEM((voxels, C), bf16),
            pltpu.VMEM((voxels + 2 * PAD, TAPS * C), bf16),
            pltpu.VMEM((voxels + 2 * PAD, TAPS * C), bf16),
            pltpu.VMEM((C, voxels), bf16),
            pltpu.VMEM((C, voxels), bf16),
            pltpu.VMEM((2, C, 9 * C), f32),
            pltpu.VMEM((2, 9, 1, LAYER), jnp.int32),
            pltpu.VMEM((2, LAYER, C), bf16),
            pltpu.VMEM((2, LAYER, C), bf16),
            pltpu.VMEM((TAPS, C, C), bf16),
            pltpu.VMEM((n_space, TAPS, chunk, C), bf16),
            pltpu.VMEM((SIDE, TAPS, chunk, C), bf16),
            pltpu.VMEM((SIDE, TAPS, chunk, C), bf16),
            pltpu.VMEM((TAPS, chunk, C), bf16),
            dma((4,)),
            dma((2, 3)),
            dma((2, 3)),
            dma((GROUPS,)),
            dma((GROUPS,)),
            dma((GROUPS,)),
            dma((GROUPS,)),
            dma((GROUPS,)),
            dma((GROUPS,)),
            dma((GROUPS,)),
            dma((GROUPS,)),
            dma((2, 8)),
            dma((GROUPS, AXES)),
        ],
        compiler_params=pltpu.CompilerParams(
            vmem_limit_bytes=61 * 2**20, collective_id=0, has_side_effects=True
        ),
        name="sparse_conv",
    )(features[0], jnp.transpose(neighbours, (1, 0, 2)), weight, grad_out[0])
    norm = 1.0 / math.sqrt(n_dp * n_space * voxels)
    conv, gin, gw = pl.pallas_call(
        functools.partial(finish_kernel, norm=norm),
        out_shape=(
            jax.ShapeDtypeStruct((voxels, C), bf16),
            jax.ShapeDtypeStruct((voxels, C), bf16),
            jax.ShapeDtypeStruct((TAPS, C, C), f32),
        ),
        in_specs=[pl.BlockSpec(memory_space=pltpu.HBM)] * 3,
        out_specs=(anywhere,) * 3,
        scratch_shapes=[
            pltpu.VMEM((voxels, C), bf16),
            pltpu.VMEM((voxels, C), bf16),
            pltpu.VMEM((TAPS, C, C), bf16),
            pltpu.VMEM((TAPS, C, C), f32),
            dma((7,)),
            dma((7,)),
        ],
        compiler_params=pltpu.CompilerParams(vmem_limit_bytes=61 * 2**20),
        name="scale",
    )(conv, gin, gw)
    return conv[None], gin[None], gw


def solution(mesh):
    in_specs = (P("dp", "space", None), P("dp", None, "space"), P(), P("dp", "space", None))
    out_specs = (P("dp", "space", None), P("dp", "space", None), P())
    return jax.shard_map(local, mesh=mesh, in_specs=in_specs, out_specs=out_specs, check_vma=False)
```

```python
import functools
import math

import jax
import jax.numpy as jnp
from jax import lax
from jax.experimental import pallas as pl
from jax.experimental.pallas import tpu as pltpu
from jax.sharding import PartitionSpec as P

LAYER, ROW, TAPS, C, TILE = 1024, 16, 27, 128, 128
PAD = ROW
CENTRE = TAPS // 2
AXES, SIDE = 3, 4
ORDER = tuple(range(9, 18)) + tuple(range(0, 9)) + tuple(range(18, 27))
SETS = ({1: (0, 9)}, {0: (9, 6), 1: (15, 6), 2: (21, 6)})
GROUPS = len(SETS)
bf16, f32 = jnp.bfloat16, jnp.float32
MESH = pl.DeviceIdType.MESH


def shift(k):
    return k // 9 - 1, k % 9 // 3 - 1


def one_hot(targets, first):
    local = jnp.where(targets >= 0, targets - first, -1)
    local = jnp.where((local >= 0) & (local < TILE), local, -1)
    local = local.astype(f32).astype(bf16)
    rows = lax.broadcasted_iota(jnp.int32, (TILE, TILE), 0).astype(f32).astype(bf16)
    return jnp.where(
        jnp.broadcast_to(local, (TILE, TILE)) == rows, jnp.ones((), bf16), jnp.zeros((), bf16)
    )


def scatter_tile(feats, grads, targets, first_target, row, taps, picked_f, picked_g):
    hot = [
        one_hot(targets[i], first_target + shift(k)[1] * ROW) for i, k in enumerate(taps)
    ]
    hot = jnp.concatenate(hot, 0)
    out_f = jnp.dot(hot, feats, preferred_element_type=f32).astype(bf16)
    out_g = jnp.dot(hot, grads, preferred_element_type=f32).astype(bf16)
    for i, k in enumerate(taps):
        at = pl.ds(pl.multiple_of(row + shift(k)[1] * ROW, ROW), TILE)
        picked_f[at, k * C : (k + 1) * C] = out_f[i * TILE : (i + 1) * TILE]
        picked_g[at, k * C : (k + 1) * C] = out_g[i * TILE : (i + 1) * TILE]


def kernel(
    f_hbm, n_hbm, w_hbm, g_hbm,
    conv_hbm, gin_hbm, gw_hbm,
    f_ref, g_ref, n_ref, w_ref, conv_ref, gin_ref, picked_f, picked_g, f_t, g_t,
    held, n_halo, f_halo, g_halo, part, part_in, first, second, result,
    load_sem, halo_send, halo_recv, a_send, a_recv, b_send, b_recv, c_send, c_recv, d_send, d_recv,
    out_sem, own_sem,
    *, voxels, n_space, rows,
):
    layers = voxels // LAYER
    tiles, layer_tiles = voxels // TILE, LAYER // TILE
    chunk = C // n_space
    blocks = voxels // rows
    s = lax.axis_index("space")
    q = lax.axis_index("dp")
    base = s * voxels
    x, y, z, core = lax.div(q, SIDE), lax.rem(q, SIDE), lax.div(s, 2), lax.rem(s, 2)
    pos = (z, x, y)

    def on_axis(a, i, c):
        if a == 0:
            return {"dp": q, "space": 2 * i + c}
        return {"dp": SIDE * i + y if a == 1 else SIDE * x + i, "space": 2 * z + c}

    loads = [
        pltpu.make_async_copy(src, dst, load_sem.at[i])
        for i, (src, dst) in enumerate(
            [(n_hbm, n_ref), (f_hbm, f_ref), (g_hbm, g_ref), (w_hbm, w_ref)]
        )
    ]
    for load in loads:
        load.start()

    barrier = pltpu.get_barrier_semaphore()
    pl.semaphore_signal(barrier, inc=1, device_id=on_axis(0, z, 1 - core), device_id_type=MESH)
    for a in range(AXES):
        for d in range(1, SIDE):
            for c in range(2):
                pl.semaphore_signal(
                    barrier, inc=1, device_id=on_axis(a, lax.rem(pos[a] + d, SIDE), c),
                    device_id_type=MESH,
                )
    peers = 1 + AXES * (SIDE - 1) * 2

    for row in (0, ROW, voxels + PAD - LAYER - ROW, voxels + PAD - ROW, voxels + PAD):
        picked_f[row : row + ROW, :] = jnp.zeros((ROW, TAPS * C), bf16)
        picked_g[row : row + ROW, :] = jnp.zeros((ROW, TAPS * C), bf16)

    def halo_copies(side):
        peer = s + 1 if side == 0 else s - 1
        at = pl.ds(voxels - LAYER if side == 0 else 0, LAYER)
        return [
            pltpu.make_async_remote_copy(
                src_ref=src, dst_ref=dst, send_sem=halo_send.at[side, i],
                recv_sem=halo_recv.at[side, i], device_id={"space": peer}, device_id_type=MESH,
            )
            for i, (src, dst) in enumerate(
                [
                    (n_hbm.at[pl.ds(18 if side == 0 else 0, 9), :, at], n_halo.at[side]),
                    (f_hbm.at[at], f_halo.at[side]),
                    (g_hbm.at[at], g_halo.at[side]),
                ]
            )
        ]

    halos = [halo_copies(0), halo_copies(1)]
    has = [s < n_space - 1, s > 0]

    for side in (0, 1):

        @pl.when(jnp.logical_not(has[1 - side]))
        def _():
            n_halo[side] = jnp.full(n_halo.shape[1:], -1, jnp.int32)
            f_halo[side] = jnp.zeros(f_halo.shape[1:], bf16)
            g_halo[side] = jnp.zeros(g_halo.shape[1:], bf16)

    def each(count, body):
        for t in range(count):
            body(t)

    def own(t, taps):
        start = t * TILE
        at = pl.ds(start, TILE)
        dz = shift(taps[0])[0]
        scatter_tile(
            f_ref[at, :], g_ref[at, :], n_ref[taps[0] : taps[-1] + 1, :, at],
            base + start + dz * LAYER, start + PAD + dz * LAYER, taps, picked_f, picked_g,
        )

    def centre(t):
        start = t * TILE
        at, to = pl.ds(start, TILE), pl.ds(start + PAD, TILE)
        lanes = slice(CENTRE * C, (CENTRE + 1) * C)
        feats, grads = f_ref[at, :], g_ref[at, :]
        picked_f[to, lanes] = feats
        picked_g[to, lanes] = grads
        f_t[:, at] = feats.T
        g_t[:, at] = grads.T

    def from_halo(side):
        dz, layer = (1, 0) if side == 0 else (-1, layers - 1)
        taps = range(9 * (dz + 1), 9 * (dz + 1) + 9)

        @pl.when(has[1 - side])
        def _():
            for copy in halos[side]:
                copy.wait_recv()

        def body(t):
            start = t * TILE
            at = pl.ds(start, TILE)
            scatter_tile(
                f_halo[side, at, :], g_halo[side, at, :], n_halo[side, :, :, at],
                base + layer * LAYER + start, start + PAD + layer * LAYER, taps,
                picked_f, picked_g,
            )

        each(layer_tiles, body)

    near = voxels - LAYER

    def products(k, count, begin, end):
        at, rows_in, here = slice(k * C, (k + count) * C), slice(PAD + begin, PAD + end), slice(begin, end)
        return (
            jnp.dot(f_t[:, here], picked_g[rows_in, at], preferred_element_type=f32),
            jnp.dot(g_t[:, here], picked_f[rows_in, at], preferred_element_type=f32),
        )

    def put(k, count, straight, mirrored):
        for c in range(count):
            lanes = slice(c * C, (c + 1) * C)
            part[ORDER.index(k + c)] = straight[:, lanes].astype(bf16)
            if mirrored is not None:
                part[ORDER.index(TAPS - 1 - k - c)] = mirrored[:, lanes].T.astype(bf16)

    parts_below = ((0, 4), (4, 4), (8, 1))

    def weight_grad_same():
        put(9, 4, *products(9, 4, 0, voxels))
        put(CENTRE, 1, jnp.dot(f_t[...], g_ref[...], preferred_element_type=f32), None)

    def weight_grad_near():
        for k, count in parts_below:
            lanes = slice(k * C, (k + count) * C)
            held[0, :, lanes], held[1, :, lanes] = products(k, count, 0, near)

    def weight_grad_far():
        for k, count in parts_below:
            lanes = slice(k * C, (k + count) * C)
            straight, mirrored = products(k, count, near, voxels)
            put(k, count, held[0, :, lanes] + straight, held[1, :, lanes] + mirrored)

    line = [2 * p + core for p in pos]

    def taps_of(g, a):
        return pl.ds(*SETS[g][a])

    def ring(i, n):
        return lax.rem(i, n)

    def rows_of(i):
        return pl.ds(pl.multiple_of(i * chunk, chunk), chunk)

    def on_line(a, i):
        return on_axis(a, lax.div(i, 2), lax.rem(i, 2))

    def a_copy(g, a, d):
        to = ring(line[a] + d, n_space)
        return pltpu.make_async_remote_copy(
            src_ref=part.at[taps_of(g, a), rows_of(to)], dst_ref=part_in.at[d, taps_of(g, a)],
            send_sem=a_send.at[g], recv_sem=a_recv.at[g],
            device_id=on_line(a, to), device_id_type=MESH,
        )

    def axis_copy(values, send, recv, g, a, b, d):
        here = values.at[pos[b], taps_of(g, a)]
        return pltpu.make_async_remote_copy(
            src_ref=here, dst_ref=here, send_sem=send.at[g], recv_sem=recv.at[g],
            device_id=on_axis(b, ring(pos[b] + d, SIDE), core), device_id_type=MESH,
        )

    def b_copy(g, a, d):
        return axis_copy(first, b_send, b_recv, g, a, (a + 1) % AXES, d)

    def c_copy(g, a, d):
        return axis_copy(second, c_send, c_recv, g, a, (a + 2) % AXES, d)

    def d_copy(g, a, d):
        return pltpu.make_async_remote_copy(
            src_ref=result.at[taps_of(g, a)], dst_ref=gw_hbm.at[taps_of(g, a), rows_of(line[a])],
            send_sem=d_send.at[g], recv_sem=d_recv.at[g],
            device_id=on_line(a, ring(line[a] + d, n_space)), device_id_type=MESH,
        )

    def own_rows(g, a):
        return pltpu.make_async_copy(
            result.at[taps_of(g, a)], gw_hbm.at[taps_of(g, a), rows_of(line[a])], own_sem.at[g, a]
        )

    def wait_all(values, g, sem):
        start = min(at for at, _ in SETS[g].values())
        count = sum(n for _, n in SETS[g].values())
        held_by = values.at[pl.ds(1, values.shape[0] - 1), pl.ds(start, count)]
        pltpu.make_async_copy(held_by, held_by, sem.at[g]).wait()

    def each_tap(g, a, body):
        for i in range(SETS[g][a][1]):
            body(SETS[g][a][0] + i)

    def stage_a(g):
        for d in range(1, n_space):
            for a in SETS[g]:
                a_copy(g, a, d).start()

    def stage_b(g):
        wait_all(part_in, g, a_recv)
        for a in SETS[g]:

            def add(k):
                total = part[k, rows_of(line[a]), :].astype(f32)
                for d in range(1, n_space):
                    total = total + part_in[d, k].astype(f32)
                first[pos[(a + 1) % AXES], k] = total.astype(bf16)

            each_tap(g, a, add)
            for d in range(1, SIDE):
                b_copy(g, a, d).start()

    def added(values, k):
        total = values[0, k].astype(f32)
        for i in range(1, SIDE):
            total = total + values[i, k].astype(f32)
        return total.astype(bf16)

    def stage_c(g):
        wait_all(first, g, b_recv)
        for a in SETS[g]:

            def add(k):
                second[pos[(a + 2) % AXES], k] = added(first, k)

            each_tap(g, a, add)
            for d in range(1, SIDE):
                c_copy(g, a, d).start()

    def stage_d(g):
        wait_all(second, g, c_recv)
        for a in SETS[g]:

            def add(k):
                result[k] = added(second, k)

            each_tap(g, a, add)
            for d in range(1, n_space):
                d_copy(g, a, d).start()
            own_rows(g, a).start()

    def sent(g):
        wait_all(part_in, g, a_send)
        wait_all(first, g, b_send)
        wait_all(second, g, c_send)

    def finish(g):
        for a in SETS[g]:
            own_rows(g, a).wait()
        wait_all(part_in, g, d_send)
        wait_all(part_in, g, d_recv)

    pl.semaphore_wait(barrier, peers)
    for side in (1, 0):

        @pl.when(has[side])
        def _():
            for copy in halos[side]:
                copy.start()

    for load in loads[:3]:
        load.wait()

    def first_taps(t):
        centre(t)
        own(t, range(9, 13))

    each(tiles, first_taps)
    weight_grad_same()
    stage_a(0)
    each(tiles - layer_tiles, lambda t: own(t + layer_tiles, range(0, 9)))
    weight_grad_near()
    stage_b(0)
    from_halo(1)
    weight_grad_far()
    stage_a(1)
    each(tiles, lambda t: own(t, range(14, 18)))
    each(tiles - layer_tiles, lambda t: own(t, range(18, 27)))
    stage_b(1)
    stage_c(0)
    from_halo(0)
    loads[3].wait()

    def conv(i):
        start = i * rows
        taps_in = jnp.concatenate([w_ref[TAPS - 1 - k] for k in range(TAPS)], 0)
        conv_ref[pl.ds(start, rows), :] = jnp.dot(
            picked_f[pl.ds(start + PAD, rows), :], taps_in, preferred_element_type=f32
        ).astype(bf16)

    def gin(i):
        start = i * rows
        taps_out = jnp.concatenate([w_ref[k] for k in range(TAPS)], 1)
        gin_ref[pl.ds(start, rows), :] = lax.dot_general(
            picked_g[pl.ds(start + PAD, rows), :], taps_out, (((1,), (1,)), ((), ())),
            preferred_element_type=f32,
        ).astype(bf16)

    def out_copy(src, dst, which, i):
        at = pl.ds(i * rows, rows)
        return pltpu.make_async_copy(src.at[at], dst.at[at], out_sem.at[which, i])

    steps = [(conv, conv_ref, conv_hbm, 0, i) for i in range(blocks)]
    steps += [(gin, gin_ref, gin_hbm, 1, i) for i in range(blocks)]
    for step, (make, src, dst, which, i) in enumerate(steps):
        make(i)
        if step != 0 and step != blocks + 1:
            out_copy(src, dst, which, i).start()
        if step == 1:
            out_copy(conv_ref, conv_hbm, 0, 0).start()
            stage_c(1)
            stage_d(0)
        if step == blocks:
            stage_d(1)
    out_copy(gin_ref, gin_hbm, 1, 1).start()

    for side in (0, 1):

        @pl.when(has[side])
        def _():
            for copy in halos[side]:
                copy.wait_send()

    for g in range(GROUPS):
        sent(g)
    for i in range(blocks):
        out_copy(conv_ref, conv_hbm, 0, i).wait()
        out_copy(gin_ref, gin_hbm, 1, i).wait()
    for g in range(GROUPS):
        finish(g)


def finish_kernel(
    conv_in, gin_in, gw_in, conv_out, gin_out, gw_out, conv, gin, raw, scaled, in_sem, out_sem, *, norm
):
    voxels = conv.shape[0]
    pieces = []
    for i in range(0, TAPS, 9):
        taps, out = pl.ds(i, 9), pl.ds(ORDER[i], 9)
        pieces.append((gw_in.at[taps], raw.at[taps], scaled.at[taps], gw_out.at[out]))
    for src, held, dst in ((conv_in, conv, conv_out), (gin_in, gin, gin_out)):
        for i in range(2):
            half = pl.ds(i * (voxels // 2), voxels // 2)
            pieces.append((src.at[half], held.at[half], held.at[half], dst.at[half]))
    ins = [pltpu.make_async_copy(p[0], p[1], in_sem.at[i]) for i, p in enumerate(pieces)]
    outs = [pltpu.make_async_copy(p[2], p[3], out_sem.at[i]) for i, p in enumerate(pieces)]
    for copy in ins:
        copy.start()
    for i in range(len(pieces)):
        ins[i].wait()
        if i < TAPS // 9:
            scaled[9 * i : 9 * i + 9] = raw[9 * i : 9 * i + 9].astype(f32) * norm
        outs[i].start()
    for copy in outs:
        copy.wait()


def local(features, neighbours, weight, grad_out):
    voxels = features.shape[1]
    n_dp, n_space = lax.axis_size("dp"), lax.axis_size("space")
    chunk = C // n_space
    dma = pltpu.SemaphoreType.DMA
    anywhere = pl.BlockSpec(memory_space=pl.ANY)
    conv, gin, gw = pl.pallas_call(
        functools.partial(
            kernel, voxels=voxels, n_space=n_space, rows=1024
        ),
        out_shape=(
            jax.ShapeDtypeStruct((voxels, C), bf16),
            jax.ShapeDtypeStruct((voxels, C), bf16),
            jax.ShapeDtypeStruct((TAPS, C, C), bf16),
        ),
        in_specs=[anywhere] * 4,
        out_specs=(anywhere,) * 3,
        scratch_shapes=[
            pltpu.VMEM((voxels, C), bf16),
            pltpu.VMEM((voxels, C), bf16),
            pltpu.VMEM((TAPS, 1, voxels), jnp.int32),
            pltpu.VMEM((TAPS, C, C), bf16),
            pltpu.VMEM((voxels, C), bf16),
            pltpu.VMEM((voxels, C), bf16),
            pltpu.VMEM((voxels + 2 * PAD, TAPS * C), bf16),
            pltpu.VMEM((voxels + 2 * PAD, TAPS * C), bf16),
            pltpu.VMEM((C, voxels), bf16),
            pltpu.VMEM((C, voxels), bf16),
            pltpu.VMEM((2, C, 9 * C), f32),
            pltpu.VMEM((2, 9, 1, LAYER), jnp.int32),
            pltpu.VMEM((2, LAYER, C), bf16),
            pltpu.VMEM((2, LAYER, C), bf16),
            pltpu.VMEM((TAPS, C, C), bf16),
            pltpu.VMEM((n_space, TAPS, chunk, C), bf16),
            pltpu.VMEM((SIDE, TAPS, chunk, C), bf16),
            pltpu.VMEM((SIDE, TAPS, chunk, C), bf16),
            pltpu.VMEM((TAPS, chunk, C), bf16),
            dma((4,)),
            dma((2, 3)),
            dma((2, 3)),
            dma((GROUPS,)),
            dma((GROUPS,)),
            dma((GROUPS,)),
            dma((GROUPS,)),
            dma((GROUPS,)),
            dma((GROUPS,)),
            dma((GROUPS,)),
            dma((GROUPS,)),
            dma((2, 8)),
            dma((GROUPS, AXES)),
        ],
        compiler_params=pltpu.CompilerParams(
            vmem_limit_bytes=61 * 2**20, collective_id=0, has_side_effects=True
        ),
        name="sparse_conv",
    )(features[0], jnp.transpose(neighbours, (1, 0, 2)), weight, grad_out[0])
    norm = 1.0 / math.sqrt(n_dp * n_space * voxels)
    conv, gin, gw = pl.pallas_call(
        functools.partial(finish_kernel, norm=norm),
        out_shape=(
            jax.ShapeDtypeStruct((voxels, C), bf16),
            jax.ShapeDtypeStruct((voxels, C), bf16),
            jax.ShapeDtypeStruct((TAPS, C, C), f32),
        ),
        in_specs=[pl.BlockSpec(memory_space=pltpu.HBM)] * 3,
        out_specs=(anywhere,) * 3,
        scratch_shapes=[
            pltpu.VMEM((voxels, C), bf16),
            pltpu.VMEM((voxels, C), bf16),
            pltpu.VMEM((TAPS, C, C), bf16),
            pltpu.VMEM((TAPS, C, C), f32),
            dma((7,)),
            dma((7,)),
        ],
        compiler_params=pltpu.CompilerParams(vmem_limit_bytes=61 * 2**20),
        name="scale",
    )(conv, gin, gw)
    return conv[None], gin[None], gw


def solution(mesh):
    in_specs = (P("dp", "space", None), P("dp", None, "space"), P(), P("dp", "space", None))
    out_specs = (P("dp", "space", None), P("dp", "space", None), P())
    return jax.shard_map(local, mesh=mesh, in_specs=in_specs, out_specs=out_specs, check_vma=False)
```
